32 devices in a mesh: snode: 8 (over z, x), col: 4 (over y, core).
Axes of the slice: x: 2, y: 2, z: 4, core: 2. Of those that a mesh axis runs over, the one named last changes fastest.
Arguments:
- rhs: float32 [3, 8192, 256], P(None, ('snode', 'col')), may hold values from -6 to 6
- dinv: bfloat16 [3, 8192, 1024], P(None, ('snode', 'col')), may hold values from -2 to 2, as said below
- loff: bfloat16 [2, 65536, 1024], P(None, ('snode', 'col')), may hold values from -0.046875 to 0.046875
- targets: int32 [2, 512], P(None, ('snode', 'col')), may hold values from 0 to 15, as said below
Outputs:
- solution: float32 [3, 8192, 256], P(None, ('snode', 'col'))
The draws below stay inside these ranges and needn't reach their ends.
Inputs may be any that keep to these rules, and one draw needn't show every extreme that they name: `targets`: the 16 entries that one device holds for one level are distinct. `dinv`: each block is the inverse of a lower-triangular block: lower triangular, with diagonal entries from 0.5 to 2.
All inputs are finite; a program needn't handle non-finite values.
Results may differ from the reference program's by a relative error of at most 0.025.
Values may be sent and summed in bfloat16 or wider, within the bound.
A program may use at most 64 MiB of HBM per device.

```python
import math
import jax
import jax.numpy as jnp
from jax import lax

W = 1024
BLK = 128
NRHS = 256
LEVELS = 3
OFF_DEV = 16
TARGETS = 16
NROWS = 8192
NLINKS = 512
NOFF = 65536
N_SNODE = 8
N_COL = 4


def draw_targets(key, part):
    count = (LEVELS - 1) * NLINKS // OFF_DEV
    keys = jax.random.split(key, count)
    picks = jax.vmap(lambda single_key: jax.random.permutation(single_key, TARGETS)[:OFF_DEV])(keys)
    return picks.reshape(LEVELS - 1, NLINKS).astype(jnp.int32)


def draw_dinv(key, part):
    key_diag, key_off = jax.random.split(jax.random.fold_in(key, 7))
    shape = (LEVELS, NROWS, W)
    row_index = lax.broadcasted_iota(jnp.int32, shape, 1) % W
    col_index = lax.broadcasted_iota(jnp.int32, shape, 2)
    below = 1.5 * jax.random.normal(key_off, shape, jnp.float32) / math.sqrt(W)
    diagonal = jnp.exp(jax.random.uniform(key_diag, shape, jnp.float32, math.log(0.5), math.log(2.0)))
    values = jnp.where(col_index < row_index, below, jnp.where(col_index == row_index, diagonal, 0.0))
    return values.astype(jnp.bfloat16)


def block_levels(stream_key, shape, pieces, low, top_value):
    def one(axis_at, blocks):
        steps = jax.random.uniform(jax.random.fold_in(jax.random.fold_in(stream_key, 6), axis_at), (blocks,), jnp.float32, low / len(pieces), top_value / len(pieces))
        return jnp.repeat(jnp.exp(steps), shape[axis_at] // blocks).reshape((-1,) + (1,) * (len(shape) - axis_at - 1))

    gain = one(*pieces[0])
    for cut in pieces[1:]:
        gain = gain * one(*cut)
    return gain


def noise(own_key, shape, deviation, limit, cuts=(), dtype=jnp.bfloat16):
    array = deviation * jax.random.normal(own_key, shape, jnp.float32)
    if cuts:
        array = array * block_levels(own_key, shape, cuts, -0.22, 0.18)
    return jnp.clip(array, -limit, limit).astype(dtype)


def setup_inputs(seed: int = 0) -> dict:
    key_of = jax.random.split(jax.random.key(seed), 5)
    rhs = noise(key_of[0], (LEVELS, NROWS, NRHS), 1.0, 6.0, ((1, 32),), jnp.float32)
    dinv = draw_dinv(jax.random.fold_in(key_of[4], 71), 0)
    loff = noise(key_of[2], (LEVELS - 1, NOFF, W), (W * OFF_DEV) ** -0.5, 0.046875, ((1, 32),))
    targets = draw_targets(jax.random.fold_in(key_of[4], 71), 0)
    return {"rhs": rhs, "dinv": dinv, "loff": loff, "targets": targets}


def diag_apply(inverse_level, vector_bf, transpose):
    blocks = inverse_level.reshape(N_SNODE, W, W)
    vectors = vector_bf.reshape(N_SNODE, W, NRHS)

    def single(pair):
        matrix, vector = pair
        if transpose:
            return jnp.dot(matrix.T, vector, preferred_element_type=jnp.float32)
        return jnp.dot(matrix, vector, preferred_element_type=jnp.float32)

    return lax.map(single, (blocks, vectors)).reshape(NROWS, NRHS)


def spread(loff_level, links, solved_bf, per_col):
    blocks = loff_level.reshape(N_SNODE, N_COL * OFF_DEV * BLK, W)
    solved = solved_bf.reshape(N_SNODE, W, NRHS)
    dest = links.reshape(N_SNODE, N_COL * OFF_DEV)
    col_index = (jnp.arange(N_COL * OFF_DEV) // OFF_DEV).astype(jnp.int32)

    def advance(running, item):
        blocks_here, solved_here, target = item
        update = jnp.dot(blocks_here, solved_here, preferred_element_type=jnp.float32).astype(jnp.bfloat16)
        update = lax.optimization_barrier(update)
        update = update.astype(jnp.float32).reshape(N_COL * OFF_DEV, BLK, NRHS)
        running = running.at[target // per_col, col_index, target % per_col].add(update)
        return running, None

    initial = jnp.zeros((N_SNODE, N_COL, per_col, BLK, NRHS), jnp.float32)
    running, unused = lax.scan(advance, initial, (blocks, solved, dest))
    return running.reshape(NROWS, NRHS)


def gather_back(loff_level, links, upper_bf, per_col):
    blocks = loff_level.reshape(N_SNODE, N_COL * OFF_DEV * BLK, W)
    upper = upper_bf.reshape(N_SNODE, N_COL, per_col, BLK, NRHS)
    dest = links.reshape(N_SNODE, N_COL, OFF_DEV)
    col_index = lax.broadcasted_iota(jnp.int32, (N_COL, OFF_DEV), 0)

    def single(pair):
        blocks_here, target = pair
        picked = upper[target // per_col, col_index, target % per_col]
        picked = picked.reshape(N_COL * OFF_DEV * BLK, NRHS)
        return jnp.dot(blocks_here.T, picked, preferred_element_type=jnp.float32)

    return lax.map(single, (blocks, dest)).reshape(NROWS, NRHS)


def reference(rhs, dinv, loff, targets):
    per_col = W // BLK // N_COL
    incoming = jnp.zeros((NROWS, NRHS), jnp.float32)
    forward = []
    for level in range(LEVELS):
        resid_bf = (rhs[level] - incoming).astype(jnp.bfloat16)
        solved = diag_apply(dinv[level], resid_bf, False)
        forward.append(solved)
        if level + 1 < LEVELS:
            incoming = spread(loff[level], targets[level], solved.astype(jnp.bfloat16), per_col)
    results = [None] * LEVELS
    upper_bf = None
    for level in reversed(range(LEVELS)):
        reduced = forward[level]
        if level + 1 < LEVELS:
            reduced = reduced - gather_back(loff[level], targets[level], upper_bf, per_col)
        solved = diag_apply(dinv[level], reduced.astype(jnp.bfloat16), True)
        results[level] = solved
        upper_bf = solved.astype(jnp.bfloat16)
    return jnp.stack(results)
```

```python
import jax
import jax.numpy as jnp
from jax import lax
from jax.experimental import pallas as pl
from jax.experimental.pallas import tpu as pltpu
from jax.sharding import PartitionSpec as P

BLK = 128


def solve_block(matrix, resid_bf):
    return jnp.dot(
        matrix,
        lax.all_gather(resid_bf, "col", axis=0, tiled=True),
        preferred_element_type=jnp.float32,
    )


def route(update, links, col_rows):
    groups = lax.axis_size("snode")
    rhs_count = update.shape[1]
    flat = update.reshape(links.shape[0], BLK * rhs_count)
    count = groups * col_rows
    number = count // BLK
    wanted = 0 // BLK + lax.iota(jnp.int32, number)
    select = (wanted[:, None] == links[None, :]).astype(jnp.bfloat16)
    outgoing = (
        jnp.dot(select, flat, preferred_element_type=jnp.float32)
        .reshape(count, rhs_count)
        .astype(jnp.bfloat16)
        .reshape(groups, col_rows, rhs_count)
    )
    arrived = lax.all_to_all(outgoing, "snode", split_axis=0, concat_axis=0, tiled=True)
    return jnp.sum(arrived.astype(jnp.float32), axis=0)


def fetch(upper_bf, links):
    rhs_count = upper_bf.shape[1]
    gathered = lax.all_gather(upper_bf, "snode", axis=0, tiled=True)
    number = gathered.shape[0] // BLK
    wanted = lax.iota(jnp.int32, number)
    select = (links[:, None] == wanted[None, :]).astype(jnp.bfloat16)
    picked = jnp.dot(
        select, gathered.reshape(number, BLK * rhs_count), preferred_element_type=jnp.float32
    )
    return picked.astype(jnp.bfloat16).reshape(links.shape[0] * BLK, rhs_count)


def back_term(blocks, picked, col_rows):
    contract = (((0,), (0,)), ((), ()))

    def term(start, count):
        return lax.dot_general(blocks, picked, contract, preferred_element_type=jnp.float32)

    return lax.psum_scatter(
        term(jnp.int32(0), col_rows * lax.axis_size("col")).astype(jnp.bfloat16),
        "col",
        scatter_dimension=0,
        tiled=True,
    ).astype(jnp.float32)


def back_solve(matrix, reduced_bf, col_rows):
    contract = (((0,), (0,)), ((), ()))

    def term(start, count):
        return lax.dot_general(matrix, reduced_bf, contract, preferred_element_type=jnp.float32)

    return lax.psum_scatter(
        term(jnp.int32(0), col_rows * lax.axis_size("col")).astype(jnp.bfloat16),
        "col",
        scatter_dimension=0,
        tiled=True,
    ).astype(jnp.float32)


def body(rhs, dinv, loff, targets):
    levels = rhs.shape[0]
    col_rows = rhs.shape[1]
    rhs_count = rhs.shape[2]
    incoming = jnp.zeros((col_rows, rhs_count), jnp.float32)
    forward = []
    for level in range(levels):
        resid_bf = (rhs[level] - incoming).astype(jnp.bfloat16)
        solved = solve_block(dinv[level], resid_bf)
        forward.append(solved)
        if level + 1 < levels:
            solved_bf = solved.astype(jnp.bfloat16)
            full_bf = lax.all_gather(solved_bf, "col", axis=0, tiled=True)
            update = jnp.dot(loff[level], full_bf, preferred_element_type=jnp.float32).astype(
                jnp.bfloat16
            )
            incoming = route(update, targets[level], col_rows)
    outputs = [None] * levels
    upper_bf = None
    for level in reversed(range(levels)):
        reduced = forward[level]
        if level + 1 < levels:
            picked = fetch(upper_bf, targets[level])
            reduced = reduced - back_term(loff[level], picked, col_rows)
        solved = back_solve(dinv[level], reduced.astype(jnp.bfloat16), col_rows)
        outputs[level] = solved
        upper_bf = solved.astype(jnp.bfloat16)
    return jnp.stack(outputs)


NZ = 4
MESH_ID = pl.DeviceIdType.MESH
SENDS = 112
OFFSET = 3.0


def dot32(a, b):
    return jnp.dot(a, b, preferred_element_type=jnp.float32)


def fused_kernel(
    targets_ref,
    rhs_hbm,
    dinv_hbm,
    loff_hbm,
    out_hbm,
    rhs_v,
    d_v,
    loff_0,
    loff_1,
    r_v,
    f_v,
    fwd_own,
    fwd_all,
    own_u,
    xsend,
    xrecv,
    zsend,
    zrecv,
    up_v,
    upx_v,
    acc,
    csend,
    crecv,
    ysend,
    yrecv,
    out_v,
    inv_ref,
    local_sem,
    send_sem,
    recv_sem,
):
    bf = jnp.bfloat16
    rows = rhs_v.shape[1]
    half = r_v.shape[4]
    width = d_v.shape[3]
    s = lax.axis_index("snode")
    c = lax.axis_index("col")
    z, x = lax.div(s, 2), lax.rem(s, 2)
    y, k = lax.div(c, 2), lax.rem(c, 2)
    c_y = (1 - y) * 2 + k
    c_core = y * 2 + 1 - k
    c_diag = (1 - y) * 2 + 1 - k
    y_peer = (s, c_y)
    core_peer = (s, c_core)
    x_peer = (z * 2 + 1 - x, c)

    def z_at(d):
        return lax.rem(z + d, NZ)

    def z_peer(d):
        return (z_at(d) * 2 + x, c)

    loads = []

    def load(src, dst):
        copy = pltpu.make_async_copy(src, dst, local_sem.at[len(loads)])
        copy.start()
        loads.append(copy)
        return copy

    load_rhs = load(rhs_hbm, rhs_v)
    load_d = [None] * 3
    load_loff = [None] * 2
    load_d[0] = load(dinv_hbm.at[0], d_v.at[0, c])
    load_loff[0] = load(loff_hbm.at[0], loff_0)
    load_d[1] = load(dinv_hbm.at[1], d_v.at[1, c])
    load_loff[1] = load(loff_hbm.at[1], loff_1)
    load_d[2] = load(dinv_hbm.at[2], d_v.at[2, c])

    barrier = pltpu.get_barrier_semaphore()
    peers = [y_peer, core_peer, x_peer, z_peer(1), z_peer(2), z_peer(3)]
    for peer in peers:
        pl.semaphore_signal(barrier, inc=1, device_id=peer, device_id_type=MESH_ID)
    load_rhs.wait()
    for h in range(2):
        r_v[h, 0, c] = rhs_v[0, :, h * half : (h + 1) * half].astype(bf)
    pl.semaphore_wait(barrier, len(peers))

    sent = []
    stores = []

    def remote(src, dst, peer):
        at = len(sent)
        copy = pltpu.make_async_remote_copy(
            src_ref=src,
            dst_ref=dst,
            send_sem=send_sem.at[at],
            recv_sem=recv_sem.at[at],
            device_id=peer,
            device_id_type=MESH_ID,
        )
        copy.start()
        sent.append(copy)
        return copy

    def gather_start(buf):
        to_y = remote(buf.at[c], buf.at[c], y_peer)
        to_core = remote(buf.at[c], buf.at[c], core_peer)
        return to_y, to_core

    def gather_relay(buf, started):
        started[0].wait_recv()
        return remote(buf.at[c_y], buf.at[c_y], core_peer)

    def gather_end(started, relay):
        started[1].wait_recv()
        relay.wait_recv()

    def full(buf):
        return buf[...].reshape(4 * rows, half)

    def invert():
        links = inv_ref.shape[1]
        for level in range(2):
            entries = [targets_ref[level, at] for at in range(links)]
            for row in range(links):
                found = jnp.int32(0)
                for at, entry in enumerate(entries):
                    found = jnp.where(entry == row, jnp.int32(at), found)
                inv_ref[level, row] = found

    def link_rows(level, zt, xt):
        group = (zt * 2 + xt) * 2
        loff_v = (loff_0, loff_1)[level]
        first = loff_v[inv_ref[level, group]]
        second = loff_v[inv_ref[level, group + 1]]
        return jnp.concatenate([first, second], axis=0)

    def columns(level, index):
        at = pl.multiple_of(index * rows, rows)
        return d_v[level, :, :, pl.ds(at, rows)].reshape(width, rows)

    order = (2, 1, 3, 0)
    shared = {}

    def chain(h):
        lead = h == 0
        f32 = jnp.float32
        lanes = slice(h * half, (h + 1) * half)

        def gather(buf, started):
            yield 4.1
            relay = gather_relay(buf, started)
            yield 1.1
            gather_end(started, relay)

        def route_sum(level, fwd_bf):
            arrivals = {}
            for d in order:
                part = dot32(link_rows(level, z_at(d), 1 - x), fwd_bf)
                xsend[h, level, d] = part.astype(bf)
                arrivals[d] = remote(xsend.at[h, level, d], xrecv.at[h, level, d], x_peer)
            for d in order:
                own_u[h, d] = dot32(link_rows(level, z_at(d), x), fwd_bf)
            landed = []
            for d in order[:3]:
                yield 1.0
                arrivals[d].wait_recv()
                both = own_u[h, d] + xrecv[h, level, d].astype(f32)
                zsend[h, level, d] = both.astype(bf)
                landed.append(
                    remote(zsend.at[h, level, d], zrecv.at[h, level, d], z_peer(d))
                )
            yield 1.0
            arrivals[0].wait_recv()
            total = own_u[h, 0] + xrecv[h, level, 0].astype(f32)
            for at, d in enumerate(order[:3]):
                yield 3.0 if at == 0 else 1.0
                landed[at].wait_recv()
                total = total + zrecv[h, level, d].astype(f32)
            r_v[h, level + 1, c] = (rhs_v[level + 1, :, lanes] - total).astype(bf)

        started = gather_start(r_v.at[h, 0])
        if lead:
            load_d[0].wait()
            invert()
        yield from gather(r_v.at[h, 0], started)
        own = dot32(d_v[0, c], full(r_v.at[h, 0]))
        fwd_own[h, 0] = own
        f_v[h, 0, c] = own.astype(bf)
        started = gather_start(f_v.at[h, 0])
        if lead:
            load_loff[0].wait()
            load_d[1].wait()
        yield from gather(f_v.at[h, 0], started)
        if lead:
            shared[1] = gather_start(d_v.at[1])
        yield from route_sum(0, full(f_v.at[h, 0]))

        started = gather_start(r_v.at[h, 1])
        if lead:
            d_relay = gather_relay(d_v.at[1], shared[1])
        yield from gather(r_v.at[h, 1], started)
        if lead:
            gather_end(shared[1], d_relay)
        for i in range(4):
            part = dot32(d_v[1, i], full(r_v.at[h, 1]))
            fwd_all[h, i] = part
            f_v[h, 1, i] = part.astype(bf)
        if lead:
            load_d[2].wait()
            load_loff[1].wait()
            shared[2] = gather_start(d_v.at[2])
        yield from route_sum(1, full(f_v.at[h, 1]))

        started = gather_start(r_v.at[h, 2])
        if lead:
            d_relay = gather_relay(d_v.at[2], shared[2])
        fwd_own[h, 1] = fwd_all[h, c]
        yield from gather(r_v.at[h, 2], started)
        if lead:
            gather_end(shared[2], d_relay)
            shared[0] = gather_start(d_v.at[0])
        for i in range(4):
            f_v[h, 2, i] = dot32(d_v[2, i], full(r_v.at[h, 2])).astype(bf)

        def finish(level, sol_t):
            out_v[h, level] = sol_t.T
            copy = pltpu.make_async_copy(
                out_v.at[h, level],
                out_hbm.at[level, :, pl.ds(h * half, half)],
                local_sem.at[6 + 2 * level + h],
            )
            copy.start()
            stores.append(copy)

        sol_t = lax.dot_general(
            full(f_v.at[h, 2]),
            columns(2, c),
            (((0,), (0,)), ((), ())),
            preferred_element_type=f32,
        )
        for level in (1, 0):
            up_v[h, level, 0] = sol_t.astype(bf)
            own_up = up_v.at[h, level, 0]
            from_z = {}
            from_x = {0: remote(own_up, upx_v.at[h, level, 0], x_peer)}
            for d in (2, 1, 3):
                from_z[d] = remote(own_up, up_v.at[h, level, d], z_peer(d))
            finish(level + 1, sol_t)
            acc[h] = jnp.zeros((half, width), f32)
            at = pl.multiple_of(c * rows, rows)
            acc[h, :, pl.ds(at, rows)] = -(fwd_own[h, level].T)
            acc[h] += dot32(up_v[h, level, 0], link_rows(level, z, x))
            for step, d in enumerate((1, 3, 2)):
                yield 4.5 if step == 0 else 1.4
                from_z[d].wait_recv()
                from_x[d] = remote(up_v.at[h, level, d], upx_v.at[h, level, d], x_peer)
                acc[h] += dot32(up_v[h, level, d], link_rows(level, z_at(NZ - d), x))
            for d in (0, 1, 3, 2):
                yield 2.5 if d == 2 else 0.7
                from_x[d].wait_recv()
                acc[h] += dot32(upx_v[h, level, d], link_rows(level, z_at(NZ - d), 1 - x))
            if lead and level == 1:
                shared["relay"] = gather_relay(d_v.at[0], shared[0])
            if lead and level == 0:
                gather_end(shared[0], shared["relay"])
            v_bf = acc[h].astype(bf)
            csend[h, level, 0] = dot32(v_bf, columns(level, c_diag)).astype(bf)
            far = remote(csend.at[h, level, 0], crecv.at[h, level, 0], core_peer)
            csend[h, level, 1] = dot32(v_bf, columns(level, c_core)).astype(bf)
            near = remote(csend.at[h, level, 1], crecv.at[h, level, 1], core_peer)
            mine = dot32(v_bf, columns(level, c_y))
            yield 0.5
            far.wait_recv()
            ysend[h, level] = (mine + crecv[h, level, 0].astype(f32)).astype(bf)
            across = remote(ysend.at[h, level], yrecv.at[h, level], y_peer)
            mine = dot32(v_bf, columns(level, c))
            near.wait_recv()
            mine = mine + crecv[h, level, 1].astype(f32)
            yield 3.5
            across.wait_recv()
            sol_t = -(mine + yrecv[h, level].astype(f32))
        finish(0, sol_t)

    chains = [chain(0), chain(1)]
    ready = [0.0, OFFSET]
    steps = [0, 0]
    now = 0.0
    running = {0, 1}
    while running:
        pick = min(running, key=lambda h: (ready[h], h))
        if pick == 1 and 0 in running and steps[1] >= steps[0]:
            pick = 0
        now = max(now, ready[pick]) + 0.4
        steps[pick] += 1
        try:
            ready[pick] = now + next(chains[pick])
        except StopIteration:
            running.discard(pick)
    for copy in sent:
        copy.wait_send()
    for copy in stores:
        copy.wait()


def fused_body(rhs, dinv, loff, targets):
    levels, rows, count = rhs.shape
    width = dinv.shape[2]
    links = targets.shape[1]
    bf = jnp.bfloat16
    f32 = jnp.float32
    any_space = pl.BlockSpec(memory_space=pl.ANY)
    blk = (rows, count // 2)
    blk_t = (count // 2, rows)
    return pl.pallas_call(
        fused_kernel,
        out_shape=jax.ShapeDtypeStruct(rhs.shape, f32),
        in_specs=[pl.BlockSpec(memory_space=pltpu.SMEM), any_space, any_space, any_space],
        out_specs=any_space,
        scratch_shapes=[
            pltpu.VMEM((levels, rows, count), f32),
            pltpu.VMEM((levels, 4, rows, width), bf),
            pltpu.VMEM((links, BLK, width), bf),
            pltpu.VMEM((links, BLK, width), bf),
            pltpu.VMEM((2, levels, 4) + blk, bf),
            pltpu.VMEM((2, levels, 4) + blk, bf),
            pltpu.VMEM((2, 2) + blk, f32),
            pltpu.VMEM((2, 4) + blk, f32),
            pltpu.VMEM((2, 4) + blk, f32),
            pltpu.VMEM((2, 2, 4) + blk, bf),
            pltpu.VMEM((2, 2, 4) + blk, bf),
            pltpu.VMEM((2, 2, 4) + blk, bf),
            pltpu.VMEM((2, 2, 4) + blk, bf),
            pltpu.VMEM((2, 2, 4) + blk_t, bf),
            pltpu.VMEM((2, 2, 4) + blk_t, bf),
            pltpu.VMEM((2, count // 2, width), f32),
            pltpu.VMEM((2, 2, 2) + blk_t, bf),
            pltpu.VMEM((2, 2, 2) + blk_t, bf),
            pltpu.VMEM((2, 2) + blk_t, bf),
            pltpu.VMEM((2, 2) + blk_t, bf),
            pltpu.VMEM((2, levels) + blk, f32),
            pltpu.SMEM((levels - 1, links), jnp.int32),
            pltpu.SemaphoreType.DMA((12,)),
            pltpu.SemaphoreType.DMA((SENDS,)),
            pltpu.SemaphoreType.DMA((SENDS,)),
        ],
        compiler_params=pltpu.CompilerParams(
            collective_id=0, has_side_effects=True, vmem_limit_bytes=60 * 1024 * 1024
        ),
    )(targets, rhs, dinv, loff.reshape(levels - 1, links, BLK, width))


def solution(mesh):
    in_specs = (
        P(None, ("snode", "col"), None),
        P(None, ("snode", "col"), None),
        P(None, ("snode", "col"), None),
        P(None, ("snode", "col")),
    )
    out_specs = P(None, ("snode", "col"), None)
    fits = mesh.shape["snode"] == 2 * NZ and mesh.shape["col"] == 4
    return jax.shard_map(
        fused_body if fits else body,
        mesh=mesh,
        in_specs=in_specs,
        out_specs=out_specs,
        check_vma=False,
    )
```

```python
import jax
import jax.numpy as jnp
from jax import lax
from jax.experimental import pallas as pl
from jax.experimental.pallas import tpu as pltpu
from jax.sharding import PartitionSpec as P

BLK = 128


def solve_block(matrix, resid_bf):
    return jnp.dot(
        matrix,
        lax.all_gather(resid_bf, "col", axis=0, tiled=True),
        preferred_element_type=jnp.float32,
    )


def route(update, links, col_rows):
    groups = lax.axis_size("snode")
    rhs_count = update.shape[1]
    flat = update.reshape(links.shape[0], BLK * rhs_count)
    count = groups * col_rows
    number = count // BLK
    wanted = 0 // BLK + lax.iota(jnp.int32, number)
    select = (wanted[:, None] == links[None, :]).astype(jnp.bfloat16)
    outgoing = (
        jnp.dot(select, flat, preferred_element_type=jnp.float32)
        .reshape(count, rhs_count)
        .astype(jnp.bfloat16)
        .reshape(groups, col_rows, rhs_count)
    )
    arrived = lax.all_to_all(outgoing, "snode", split_axis=0, concat_axis=0, tiled=True)
    return jnp.sum(arrived.astype(jnp.float32), axis=0)


def fetch(upper_bf, links):
    rhs_count = upper_bf.shape[1]
    gathered = lax.all_gather(upper_bf, "snode", axis=0, tiled=True)
    number = gathered.shape[0] // BLK
    wanted = lax.iota(jnp.int32, number)
    select = (links[:, None] == wanted[None, :]).astype(jnp.bfloat16)
    picked = jnp.dot(
        select, gathered.reshape(number, BLK * rhs_count), preferred_element_type=jnp.float32
    )
    return picked.astype(jnp.bfloat16).reshape(links.shape[0] * BLK, rhs_count)


def back_term(blocks, picked, col_rows):
    contract = (((0,), (0,)), ((), ()))

    def term(start, count):
        return lax.dot_general(blocks, picked, contract, preferred_element_type=jnp.float32)

    return lax.psum_scatter(
        term(jnp.int32(0), col_rows * lax.axis_size("col")).astype(jnp.bfloat16),
        "col",
        scatter_dimension=0,
        tiled=True,
    ).astype(jnp.float32)


def back_solve(matrix, reduced_bf, col_rows):
    contract = (((0,), (0,)), ((), ()))

    def term(start, count):
        return lax.dot_general(matrix, reduced_bf, contract, preferred_element_type=jnp.float32)

    return lax.psum_scatter(
        term(jnp.int32(0), col_rows * lax.axis_size("col")).astype(jnp.bfloat16),
        "col",
        scatter_dimension=0,
        tiled=True,
    ).astype(jnp.float32)


def body(rhs, dinv, loff, targets):
    levels = rhs.shape[0]
    col_rows = rhs.shape[1]
    rhs_count = rhs.shape[2]
    incoming = jnp.zeros((col_rows, rhs_count), jnp.float32)
    forward = []
    for level in range(levels):
        resid_bf = (rhs[level] - incoming).astype(jnp.bfloat16)
        solved = solve_block(dinv[level], resid_bf)
        forward.append(solved)
        if level + 1 < levels:
            solved_bf = solved.astype(jnp.bfloat16)
            full_bf = lax.all_gather(solved_bf, "col", axis=0, tiled=True)
            update = jnp.dot(loff[level], full_bf, preferred_element_type=jnp.float32).astype(
                jnp.bfloat16
            )
            incoming = route(update, targets[level], col_rows)
    outputs = [None] * levels
    upper_bf = None
    for level in reversed(range(levels)):
        reduced = forward[level]
        if level + 1 < levels:
            picked = fetch(upper_bf, targets[level])
            reduced = reduced - back_term(loff[level], picked, col_rows)
        solved = back_solve(dinv[level], reduced.astype(jnp.bfloat16), col_rows)
        outputs[level] = solved
        upper_bf = solved.astype(jnp.bfloat16)
    return jnp.stack(outputs)


NZ = 4
MESH_ID = pl.DeviceIdType.MESH
SENDS = 96
ZS = (2, 1, 3)
STEPS = tuple((d, kk) for kk in range(2) for d in (2, 1, 3))
RSO = (2, 1, 3, 0)


def dot32(a, b):
    return jnp.dot(a, b, preferred_element_type=jnp.float32)


def fused_kernel(
    targets_ref,
    targets_hbm,
    rhs_hbm,
    dinv_hbm,
    loff_hbm,
    out_hbm,
    rhs_0,
    rhs_v,
    d_v,
    loff_0,
    loff_1,
    r_v,
    f_v,
    stage,
    fwd_own,
    own_u,
    xsend,
    xrecv,
    zsend,
    zrecv,
    up_v,
    upx_v,
    acc,
    ysend,
    yrecv,
    out_v,
    peer_links_v,
    peer_links,
    inv_ref,
    local_sem,
    send_sem,
    recv_sem,
):
    bf = jnp.bfloat16
    f32 = jnp.float32
    rows = rhs_0.shape[0]
    half = r_v.shape[3]
    width = d_v.shape[3]
    s = lax.axis_index("snode")
    c = lax.axis_index("col")
    z, x = lax.div(s, 2), lax.rem(s, 2)
    y, k = lax.div(c, 2), lax.rem(c, 2)
    c_y = (1 - y) * 2 + k
    c_core = y * 2 + 1 - k
    y_peer = (s, c_y)
    core_peer = (s, c_core)
    diag_peer = (s, (1 - y) * 2 + 1 - k)
    x_peer = (z * 2 + 1 - x, c)
    own = pl.ds(y * 2, 2)
    lanes = pl.ds(pl.multiple_of(k * half, half), half)
    other = pl.ds(pl.multiple_of((1 - k) * half, half), half)

    def z_at(d):
        return lax.rem(z + d, NZ)

    def z_peer(d):
        return (z_at(d) * 2 + x, c)

    loads = {}
    waited = set()

    def load(name, src, dst):
        copy = pltpu.make_async_copy(src, dst, local_sem.at[len(loads)])
        copy.start()
        loads[name] = copy

    def need(*names):
        for name in names:
            if name not in waited:
                waited.add(name)
                if name in loads:
                    loads[name].wait()
                else:
                    pushed[name].wait_recv()

    load("rhs0", rhs_hbm.at[0], rhs_0)
    load("d0", dinv_hbm.at[0], d_v.at[0, c])
    load("loff0", loff_hbm.at[0], loff_0.at[k])
    load("d1", dinv_hbm.at[1], d_v.at[1, c])
    load("rhs1", rhs_hbm.at[1, :, lanes], rhs_v.at[0, k])
    load("rhs2", rhs_hbm.at[2, :, lanes], rhs_v.at[1, k])
    load("loff1", loff_hbm.at[1], loff_1.at[k])
    load("d2", dinv_hbm.at[2], d_v.at[2, c])

    barrier = pltpu.get_barrier_semaphore()
    peers = [y_peer, core_peer, diag_peer, x_peer, z_peer(1), z_peer(2), z_peer(3)]
    for peer in peers:
        pl.semaphore_signal(barrier, inc=1, device_id=peer, device_id_type=MESH_ID)
    need("rhs0")
    r_v[0, c] = rhs_0[:, lanes].astype(bf)
    stage[...] = rhs_0[:, other].astype(bf)
    pl.semaphore_wait(barrier, len(peers))

    sent = []
    pushed = {}

    def describe(src, dst, peer):
        at = len(sent)
        copy = pltpu.make_async_remote_copy(
            src_ref=src,
            dst_ref=dst,
            send_sem=send_sem.at[at],
            recv_sem=recv_sem.at[at],
            device_id=peer,
            device_id_type=MESH_ID,
        )
        sent.append(copy)
        return copy

    def remote(src, dst, peer):
        copy = describe(src, dst, peer)
        copy.start()
        return copy

    def push(name, src, dst):
        pushed[name] = remote(src, dst, core_peer)

    def to_y(buf, kk):
        return remote(buf.at[y * 2 + kk], buf.at[y * 2 + kk], y_peer)

    def full(buf):
        return buf[...].reshape(4 * rows, half)

    def invert(level, kk, source):
        links = inv_ref.shape[2]
        entries = [source[level, at] for at in range(links)]
        for row in range(links):
            found = jnp.int32(0)
            for at, entry in enumerate(entries):
                found = jnp.where(entry == row, jnp.int32(at), found)
            inv_ref[level, kk, row] = found

    def link_rows(level, kk, zt, xt):
        group = (zt * 2 + xt) * 2
        loff_v = (loff_0, loff_1)[level]
        first = loff_v[kk, inv_ref[level, kk, group]]
        second = loff_v[kk, inv_ref[level, kk, group + 1]]
        return jnp.concatenate([first, second], axis=0)

    def columns(level, index):
        at = pl.multiple_of(index * rows, rows)
        return d_v[level, :, :, pl.ds(at, rows)].reshape(width, rows)

    first = [
        remote(r_v.at[0, c], r_v.at[0, c], y_peer),
        remote(stage, r_v.at[0, c], diag_peer),
        remote(stage, r_v.at[0, c], core_peer),
    ]
    push("d0c", dinv_hbm.at[0], d_v.at[0, c])
    push("links", targets_hbm, peer_links_v)
    push("loff0c", loff_hbm.at[0], loff_0.at[k])
    push("d1c", dinv_hbm.at[1], d_v.at[1, c])
    push("rhs1c", rhs_hbm.at[1, :, other], rhs_v.at[0, k])
    push("rhs2c", rhs_hbm.at[2, :, other], rhs_v.at[1, k])
    push("loff1c", loff_hbm.at[1], loff_1.at[k])
    push("d2c", dinv_hbm.at[2], d_v.at[2, c])

    d_y = {}
    d_relay = {}
    for level in (1, 2, 0):
        d_y[level] = describe(d_v.at[level, c], d_v.at[level, c], y_peer)
        d_relay[level] = describe(d_v.at[level, c_y], d_v.at[level, c_y], core_peer)

    def relay_d(level):
        d_y[level].wait_recv()
        d_relay[level].start()

    for level in range(2):
        invert(level, k, targets_ref)
    need("links")
    copy = pltpu.make_async_copy(peer_links_v, peer_links, local_sem.at[15])
    copy.start()
    copy.wait()
    for level in range(2):
        invert(level, 1 - k, peer_links)

    order = RSO

    def route_sum(level, fwd_bf):
        arrivals = {}
        for d in order:
            for kk in range(2):
                part = dot32(link_rows(level, kk, z_at(d), 1 - x), fwd_bf)
                xsend[level, d, kk] = part.astype(bf)
                arrivals[d, kk] = remote(
                    xsend.at[level, d, kk], xrecv.at[level, d, kk], x_peer
                )
        for d in order:
            for kk in range(2):
                own_u[d, kk] = dot32(link_rows(level, kk, z_at(d), x), fwd_bf)
        landed = {}
        for d in order[:3]:
            for kk in range(2):
                arrivals[d, kk].wait_recv()
                both = own_u[d, kk] + xrecv[level, d, kk].astype(f32)
                zsend[level, d, kk] = both.astype(bf)
                landed[d, kk] = remote(
                    zsend.at[level, d, kk], zrecv.at[level, d, kk], z_peer(d)
                )
        need("rhs%d" % (level + 1), "rhs%dc" % (level + 1))
        for kk in range(2):
            arrivals[0, kk].wait_recv()
            own_u[0, kk] += xrecv[level, 0, kk].astype(f32)
        own_u[0] = rhs_v[level] - own_u[0]
        for d in order[:2]:
            for kk in range(2):
                landed[d, kk].wait_recv()
                own_u[0, kk] -= zrecv[level, d, kk].astype(f32)
        gathers = []
        for kk in range(2):
            landed[order[2], kk].wait_recv()
            resid = own_u[0, kk] - zrecv[level, order[2], kk].astype(f32)
            r_v[level + 1, y * 2 + kk] = resid.astype(bf)
            gathers.append(to_y(r_v.at[level + 1], kk))
        return gathers

    for copy in first:
        copy.wait_recv()
    need("d0", "d0c")
    resid = full(r_v.at[0])
    gathers = []
    for kk in range(2):
        part = dot32(d_v[0, y * 2 + kk], resid)
        fwd_own[0, kk] = part
        f_v[0, y * 2 + kk] = part.astype(bf)
        gathers.append(to_y(f_v.at[0], kk))
    need("d1")
    d_y[1].start()
    need("loff0", "loff0c")
    for copy in gathers:
        copy.wait_recv()
    gathers = route_sum(0, full(f_v.at[0]))

    need("loff1", "loff1c", "d1c", "d2")
    d_y[2].start()
    relay_d(1)
    for copy in gathers:
        copy.wait_recv()
    d_relay[1].wait_recv()
    resid = full(r_v.at[1])
    for i in range(4):
        f_v[1, i] = dot32(d_v[1, i], resid).astype(bf)
    gathers = route_sum(1, full(f_v.at[1]))

    need("d2c")
    d_y[0].start()
    relay_d(2)
    resid = full(r_v.at[1])
    for kk in range(2):
        fwd_own[1, kk] = dot32(d_v[1, y * 2 + kk], resid)
    for copy in gathers:
        copy.wait_recv()
    d_relay[2].wait_recv()
    resid = full(r_v.at[2])
    for i in range(4):
        f_v[2, i] = dot32(d_v[2, i], resid).astype(bf)

    stores = []

    def finish(level, sols):
        for kk in range(2):
            out_v[level, kk] = sols[kk].T
        copy = pltpu.make_async_copy(
            out_v.at[level, k], out_hbm.at[level, :, lanes], local_sem.at[16 + level]
        )
        copy.start()
        away = remote(out_v.at[level, 1 - k], out_hbm.at[level, :, lanes], core_peer)
        stores.append((copy, away))

    from_x = {}
    from_z = {}

    def share(level, kk, sol_t):
        up_v[level, 0, kk] = sol_t.astype(bf)
        own_up = up_v.at[level, 0, kk]
        from_x[level, 0, kk] = remote(own_up, upx_v.at[level, 0, kk], x_peer)
        for d in ZS:
            from_z[level, d, kk] = remote(own_up, up_v.at[level, d, kk], z_peer(d))

    sols = []
    for kk in range(2):
        sols.append(
            lax.dot_general(
                full(f_v.at[2]),
                columns(2, y * 2 + kk),
                (((0,), (0,)), ((), ())),
                preferred_element_type=f32,
            )
        )
        share(1, kk, sols[kk])
    for level in (1, 0):
        finish(level + 1, sols)
        acc[...] = jnp.zeros((half, width), f32)
        at = pl.multiple_of(y * 2 * rows, 2 * rows)
        acc[:, pl.ds(at, 2 * rows)] = -(fwd_own[level].reshape(2 * rows, half).T)

        def gain(buf, kk, zt, xt):
            acc[...] += dot32(buf[...], link_rows(level, kk, zt, xt))

        for kk in range(2):
            gain(up_v.at[level, 0, kk], kk, z, x)
        for d, kk in STEPS:
            from_z[level, d, kk].wait_recv()
            from_x[level, d, kk] = remote(
                up_v.at[level, d, kk], upx_v.at[level, d, kk], x_peer
            )
            gain(up_v.at[level, d, kk], kk, z_at(NZ - d), x)
        if level == 0:
            relay_d(0)
        for d, kk in ((0, 0), (0, 1)) + STEPS:
            from_x[level, d, kk].wait_recv()
            gain(upx_v.at[level, d, kk], kk, z_at(NZ - d), 1 - x)
        if level == 0:
            need("d0c")
            d_relay[0].wait_recv()
        v_bf = acc[...].astype(bf)
        across = []
        for kk in range(2):
            ysend[level, kk] = dot32(v_bf, columns(level, (1 - y) * 2 + kk)).astype(bf)
            across.append(remote(ysend.at[level, kk], yrecv.at[level, kk], y_peer))
        mine = [dot32(v_bf, columns(level, y * 2 + kk)) for kk in range(2)]
        sols = []
        for kk in range(2):
            across[kk].wait_recv()
            sols.append(-(mine[kk] + yrecv[level, kk].astype(f32)))
            if level == 1:
                share(0, kk, sols[kk])
    finish(0, sols)
    for copy, away in stores:
        away.wait_recv()
        copy.wait()
    for copy in sent:
        copy.wait_send()


def fused_body(rhs, dinv, loff, targets):
    levels, rows, count = rhs.shape
    width = dinv.shape[2]
    links = targets.shape[1]
    half = count // 2
    bf = jnp.bfloat16
    f32 = jnp.float32
    any_space = pl.BlockSpec(memory_space=pl.ANY)
    pair = (2, rows, half)
    pair_t = (2, half, rows)
    return pl.pallas_call(
        fused_kernel,
        out_shape=jax.ShapeDtypeStruct(rhs.shape, f32),
        in_specs=[pl.BlockSpec(memory_space=pltpu.SMEM)] + [any_space] * 4,
        out_specs=any_space,
        scratch_shapes=[
            pltpu.VMEM((rows, count), f32),
            pltpu.VMEM((levels - 1,) + pair, f32),
            pltpu.VMEM((levels, 4, rows, width), bf),
            pltpu.VMEM((2, links, BLK, width), bf),
            pltpu.VMEM((2, links, BLK, width), bf),
            pltpu.VMEM((levels, 4, rows, half), bf),
            pltpu.VMEM((levels, 4, rows, half), bf),
            pltpu.VMEM((rows, half), bf),
            pltpu.VMEM((levels - 1,) + pair, f32),
            pltpu.VMEM((4,) + pair, f32),
            pltpu.VMEM((levels - 1, 4) + pair, bf),
            pltpu.VMEM((levels - 1, 4) + pair, bf),
            pltpu.VMEM((levels - 1, 4) + pair, bf),
            pltpu.VMEM((levels - 1, 4) + pair, bf),
            pltpu.VMEM((levels - 1, 4) + pair_t, bf),
            pltpu.VMEM((levels - 1, 4) + pair_t, bf),
            pltpu.VMEM((half, width), f32),
            pltpu.VMEM((levels - 1,) + pair_t, bf),
            pltpu.VMEM((levels - 1,) + pair_t, bf),
            pltpu.VMEM((levels,) + pair, f32),
            pltpu.VMEM((levels - 1, links), jnp.int32),
            pltpu.SMEM((levels - 1, links), jnp.int32),
            pltpu.SMEM((levels - 1, 2, links), jnp.int32),
            pltpu.SemaphoreType.DMA((20,)),
            pltpu.SemaphoreType.DMA((SENDS,)),
            pltpu.SemaphoreType.DMA((SENDS,)),
        ],
        compiler_params=pltpu.CompilerParams(
            collective_id=0, has_side_effects=True, vmem_limit_bytes=60 * 1024 * 1024
        ),
    )(targets, targets, rhs, dinv, loff.reshape(levels - 1, links, BLK, width))


def solution(mesh):
    in_specs = (
        P(None, ("snode", "col"), None),
        P(None, ("snode", "col"), None),
        P(None, ("snode", "col"), None),
        P(None, ("snode", "col")),
    )
    out_specs = P(None, ("snode", "col"), None)
    fits = mesh.shape["snode"] == 2 * NZ and mesh.shape["col"] == 4
    return jax.shard_map(
        fused_body if fits else body,
        mesh=mesh,
        in_specs=in_specs,
        out_specs=out_specs,
        check_vma=False,
    )
```

```python
import jax
import jax.numpy as jnp
from jax import lax
from jax.experimental import pallas as pl
from jax.experimental.pallas import tpu as pltpu
from jax.sharding import PartitionSpec as P

BLK = 128


def solve_block(matrix, resid_bf):
    return jnp.dot(
        matrix,
        lax.all_gather(resid_bf, "col", axis=0, tiled=True),
        preferred_element_type=jnp.float32,
    )


def route(update, links, col_rows):
    groups = lax.axis_size("snode")
    rhs_count = update.shape[1]
    flat = update.reshape(links.shape[0], BLK * rhs_count)
    count = groups * col_rows
    number = count // BLK
    wanted = 0 // BLK + lax.iota(jnp.int32, number)
    select = (wanted[:, None] == links[None, :]).astype(jnp.bfloat16)
    outgoing = (
        jnp.dot(select, flat, preferred_element_type=jnp.float32)
        .reshape(count, rhs_count)
        .astype(jnp.bfloat16)
        .reshape(groups, col_rows, rhs_count)
    )
    arrived = lax.all_to_all(outgoing, "snode", split_axis=0, concat_axis=0, tiled=True)
    return jnp.sum(arrived.astype(jnp.float32), axis=0)


def fetch(upper_bf, links):
    rhs_count = upper_bf.shape[1]
    gathered = lax.all_gather(upper_bf, "snode", axis=0, tiled=True)
    number = gathered.shape[0] // BLK
    wanted = lax.iota(jnp.int32, number)
    select = (links[:, None] == wanted[None, :]).astype(jnp.bfloat16)
    picked = jnp.dot(
        select, gathered.reshape(number, BLK * rhs_count), preferred_element_type=jnp.float32
    )
    return picked.astype(jnp.bfloat16).reshape(links.shape[0] * BLK, rhs_count)


def back_term(blocks, picked, col_rows):
    contract = (((0,), (0,)), ((), ()))

    def term(start, count):
        return lax.dot_general(blocks, picked, contract, preferred_element_type=jnp.float32)

    return lax.psum_scatter(
        term(jnp.int32(0), col_rows * lax.axis_size("col")).astype(jnp.bfloat16),
        "col",
        scatter_dimension=0,
        tiled=True,
    ).astype(jnp.float32)


def back_solve(matrix, reduced_bf, col_rows):
    contract = (((0,), (0,)), ((), ()))

    def term(start, count):
        return lax.dot_general(matrix, reduced_bf, contract, preferred_element_type=jnp.float32)

    return lax.psum_scatter(
        term(jnp.int32(0), col_rows * lax.axis_size("col")).astype(jnp.bfloat16),
        "col",
        scatter_dimension=0,
        tiled=True,
    ).astype(jnp.float32)


def body(rhs, dinv, loff, targets):
    levels = rhs.shape[0]
    col_rows = rhs.shape[1]
    rhs_count = rhs.shape[2]
    incoming = jnp.zeros((col_rows, rhs_count), jnp.float32)
    forward = []
    for level in range(levels):
        resid_bf = (rhs[level] - incoming).astype(jnp.bfloat16)
        solved = solve_block(dinv[level], resid_bf)
        forward.append(solved)
        if level + 1 < levels:
            solved_bf = solved.astype(jnp.bfloat16)
            full_bf = lax.all_gather(solved_bf, "col", axis=0, tiled=True)
            update = jnp.dot(loff[level], full_bf, preferred_element_type=jnp.float32).astype(
                jnp.bfloat16
            )
            incoming = route(update, targets[level], col_rows)
    outputs = [None] * levels
    upper_bf = None
    for level in reversed(range(levels)):
        reduced = forward[level]
        if level + 1 < levels:
            picked = fetch(upper_bf, targets[level])
            reduced = reduced - back_term(loff[level], picked, col_rows)
        solved = back_solve(dinv[level], reduced.astype(jnp.bfloat16), col_rows)
        outputs[level] = solved
        upper_bf = solved.astype(jnp.bfloat16)
    return jnp.stack(outputs)


NZ = 4
MESH_ID = pl.DeviceIdType.MESH
SENDS = 96
ZS = (1, 3, 2)
STEPS = ((1, 0), (3, 0), (1, 1), (3, 1), (2, 0), (2, 1))
RSEQ = tuple((d, kk) for d in (2, 1, 3, 0) for kk in range(2))
ZSEQ = tuple((d, kk) for d in (2, 1, 3) for kk in range(2))


def dot32(a, b):
    return jnp.dot(a, b, preferred_element_type=jnp.float32)


def fused_kernel(
    targets_ref,
    targets_hbm,
    rhs_hbm,
    dinv_hbm,
    loff_hbm,
    out_hbm,
    rhs_0,
    rhs_v,
    d_v,
    loff_0,
    loff_1,
    r_v,
    f_v,
    stage,
    fwd_own,
    own_u,
    xsend,
    xrecv,
    zsend,
    zrecv,
    up_v,
    upx_v,
    acc,
    ysend,
    yrecv,
    out_v,
    peer_links_v,
    peer_links,
    inv_ref,
    local_sem,
    send_sem,
    recv_sem,
):
    bf = jnp.bfloat16
    f32 = jnp.float32
    rows = rhs_0.shape[0]
    half = r_v.shape[3]
    width = d_v.shape[3]
    s = lax.axis_index("snode")
    c = lax.axis_index("col")
    z, x = lax.div(s, 2), lax.rem(s, 2)
    y, k = lax.div(c, 2), lax.rem(c, 2)
    c_y = (1 - y) * 2 + k
    c_core = y * 2 + 1 - k
    y_peer = (s, c_y)
    core_peer = (s, c_core)
    diag_peer = (s, (1 - y) * 2 + 1 - k)
    x_peer = (z * 2 + 1 - x, c)
    own = pl.ds(y * 2, 2)
    lanes = pl.ds(pl.multiple_of(k * half, half), half)
    other = pl.ds(pl.multiple_of((1 - k) * half, half), half)

    def z_at(d):
        return lax.rem(z + d, NZ)

    def z_peer(d):
        return (z_at(d) * 2 + x, c)

    loads = {}
    waited = set()

    def load(name, src, dst):
        copy = pltpu.make_async_copy(src, dst, local_sem.at[len(loads)])
        copy.start()
        loads[name] = copy

    def need(*names):
        for name in names:
            if name not in waited:
                waited.add(name)
                if name in loads:
                    loads[name].wait()
                else:
                    pushed[name].wait_recv()

    load("rhs0", rhs_hbm.at[0], rhs_0)
    load("d0", dinv_hbm.at[0], d_v.at[0, c])
    load("loff0", loff_hbm.at[0], loff_0.at[k])
    load("d1", dinv_hbm.at[1], d_v.at[1, c])
    load("rhs1", rhs_hbm.at[1, :, lanes], rhs_v.at[0, k])
    load("rhs2", rhs_hbm.at[2, :, lanes], rhs_v.at[1, k])
    load("loff1", loff_hbm.at[1], loff_1.at[k])
    load("d2", dinv_hbm.at[2], d_v.at[2, c])

    barrier = pltpu.get_barrier_semaphore()
    peers = [y_peer, core_peer, diag_peer, x_peer, z_peer(1), z_peer(2), z_peer(3)]
    for peer in peers:
        pl.semaphore_signal(barrier, inc=1, device_id=peer, device_id_type=MESH_ID)
    need("rhs0")
    r_v[0, c] = rhs_0[:, lanes].astype(bf)
    stage[...] = rhs_0[:, other].astype(bf)
    pl.semaphore_wait(barrier, len(peers))

    sent = []
    pushed = {}

    def describe(src, dst, peer):
        at = len(sent)
        copy = pltpu.make_async_remote_copy(
            src_ref=src,
            dst_ref=dst,
            send_sem=send_sem.at[at],
            recv_sem=recv_sem.at[at],
            device_id=peer,
            device_id_type=MESH_ID,
        )
        sent.append(copy)
        return copy

    def remote(src, dst, peer):
        copy = describe(src, dst, peer)
        copy.start()
        return copy

    def push(name, src, dst):
        pushed[name] = remote(src, dst, core_peer)

    def to_y(buf, kk):
        return remote(buf.at[y * 2 + kk], buf.at[y * 2 + kk], y_peer)

    def full(buf):
        return buf[...].reshape(4 * rows, half)

    def invert(level, kk, source):
        links = inv_ref.shape[2]
        entries = [source[level, at] for at in range(links)]
        for row in range(links):
            found = jnp.int32(0)
            for at, entry in enumerate(entries):
                found = jnp.where(entry == row, jnp.int32(at), found)
            inv_ref[level, kk, row] = found

    def link_rows(level, kk, zt, xt):
        group = (zt * 2 + xt) * 2
        loff_v = (loff_0, loff_1)[level]
        first = loff_v[kk, inv_ref[level, kk, group]]
        second = loff_v[kk, inv_ref[level, kk, group + 1]]
        return jnp.concatenate([first, second], axis=0)

    def columns(level, index):
        at = pl.multiple_of(index * rows, rows)
        return d_v[level, :, :, pl.ds(at, rows)].reshape(width, rows)

    first = [
        remote(r_v.at[0, c], r_v.at[0, c], y_peer),
        remote(stage, r_v.at[0, c], diag_peer),
        remote(stage, r_v.at[0, c], core_peer),
    ]
    push("d0c", dinv_hbm.at[0], d_v.at[0, c])
    push("links", targets_hbm, peer_links_v)
    push("loff0c", loff_hbm.at[0], loff_0.at[k])
    push("d1c", dinv_hbm.at[1], d_v.at[1, c])
    push("rhs1c", rhs_hbm.at[1, :, other], rhs_v.at[0, k])
    push("rhs2c", rhs_hbm.at[2, :, other], rhs_v.at[1, k])
    push("loff1c", loff_hbm.at[1], loff_1.at[k])
    push("d2c", dinv_hbm.at[2], d_v.at[2, c])

    d_y = {}
    d_relay = {}
    for level in (1, 2, 0):
        d_y[level] = describe(d_v.at[level, c], d_v.at[level, c], y_peer)
        d_relay[level] = describe(d_v.at[level, c_y], d_v.at[level, c_y], core_peer)

    def relay_d(level):
        d_y[level].wait_recv()
        d_relay[level].start()

    for level in range(2):
        invert(level, k, targets_ref)
    need("links")
    copy = pltpu.make_async_copy(peer_links_v, peer_links, local_sem.at[15])
    copy.start()
    copy.wait()
    for level in range(2):
        invert(level, 1 - k, peer_links)

    def route_sum(level, fwd_bf):
        arrivals = {}
        for d, kk in RSEQ:
            part = dot32(link_rows(level, kk, z_at(d), 1 - x), fwd_bf)
            xsend[level, d, kk] = part.astype(bf)
            arrivals[d, kk] = remote(xsend.at[level, d, kk], xrecv.at[level, d, kk], x_peer)
        for d, kk in RSEQ:
            own_u[d, kk] = dot32(link_rows(level, kk, z_at(d), x), fwd_bf)
        need("rhs%d" % (level + 1), "rhs%dc" % (level + 1))
        landed = {}
        for d, kk in RSEQ:
            arrivals[d, kk].wait_recv()
            both = own_u[d, kk] + xrecv[level, d, kk].astype(f32)
            if d == 0:
                own_u[0, kk] = rhs_v[level, kk] - both
                continue
            zsend[level, d, kk] = both.astype(bf)
            landed[d, kk] = remote(zsend.at[level, d, kk], zrecv.at[level, d, kk], z_peer(d))
        gathers = []
        left = [3, 3]
        for d, kk in ZSEQ:
            landed[d, kk].wait_recv()
            left[kk] -= 1
            resid = own_u[0, kk] - zrecv[level, d, kk].astype(f32)
            if left[kk]:
                own_u[0, kk] = resid
            else:
                r_v[level + 1, y * 2 + kk] = resid.astype(bf)
                gathers.append(to_y(r_v.at[level + 1], kk))
        return gathers

    for copy in first:
        copy.wait_recv()
    need("d0", "d0c")
    resid = full(r_v.at[0])
    gathers = []
    for kk in range(2):
        part = dot32(d_v[0, y * 2 + kk], resid)
        fwd_own[0, kk] = part
        f_v[0, y * 2 + kk] = part.astype(bf)
        gathers.append(to_y(f_v.at[0], kk))
    need("d1")
    d_y[1].start()
    need("loff0", "loff0c")
    for copy in gathers:
        copy.wait_recv()
    gathers = route_sum(0, full(f_v.at[0]))

    need("loff1", "loff1c", "d1c", "d2")
    d_y[2].start()
    relay_d(1)
    for copy in gathers:
        copy.wait_recv()
    d_relay[1].wait_recv()
    resid = full(r_v.at[1])
    for i in range(4):
        f_v[1, i] = dot32(d_v[1, i], resid).astype(bf)
    gathers = route_sum(1, full(f_v.at[1]))

    need("d2c")
    d_y[0].start()
    relay_d(2)
    resid = full(r_v.at[1])
    for kk in range(2):
        fwd_own[1, kk] = dot32(d_v[1, y * 2 + kk], resid)
    for copy in gathers:
        copy.wait_recv()
    d_relay[2].wait_recv()
    resid = full(r_v.at[2])
    for i in range(4):
        f_v[2, i] = dot32(d_v[2, i], resid).astype(bf)

    stores = []

    def finish(level, kk, sol_t):
        if kk == 0:
            src, dst = out_v.at[level], out_hbm.at[level, :, lanes]
            copy = pltpu.make_async_copy(src.at[k], dst, local_sem.at[16 + level])
            stores.append((copy, describe(src.at[1 - k], dst, core_peer)))
        out_v[level, kk] = sol_t.T
        copy, away = stores[-1]
        pl.when(k == kk)(copy.start)
        pl.when(k != kk)(away.start)

    from_x = {}
    from_z = {}

    def share(level, kk, sol_t):
        up_v[level, 0, kk] = sol_t.astype(bf)
        own_up = up_v.at[level, 0, kk]
        from_x[level, 0, kk] = remote(own_up, upx_v.at[level, 0, kk], x_peer)
        for d in ZS:
            from_z[level, d, kk] = remote(own_up, up_v.at[level, d, kk], z_peer(d))

    sols = []
    for kk in range(2):
        sols.append(
            lax.dot_general(
                full(f_v.at[2]),
                columns(2, y * 2 + kk),
                (((0,), (0,)), ((), ())),
                preferred_element_type=f32,
            )
        )
        share(1, kk, sols[kk])
    for level in (1, 0):
        for kk in range(2):
            finish(level + 1, kk, sols[kk])
        acc[...] = jnp.zeros((half, width), f32)
        at = pl.multiple_of(y * 2 * rows, 2 * rows)
        acc[:, pl.ds(at, 2 * rows)] = -(fwd_own[level].reshape(2 * rows, half).T)

        def gain(buf, kk, zt, xt):
            acc[...] += dot32(buf[...], link_rows(level, kk, zt, xt))

        for kk in range(2):
            gain(up_v.at[level, 0, kk], kk, z, x)
        for d, kk in STEPS:
            from_z[level, d, kk].wait_recv()
            from_x[level, d, kk] = remote(
                up_v.at[level, d, kk], upx_v.at[level, d, kk], x_peer
            )
            gain(up_v.at[level, d, kk], kk, z_at(NZ - d), x)
        if level == 0:
            relay_d(0)
        for d, kk in ((0, 0), (0, 1)) + STEPS:
            from_x[level, d, kk].wait_recv()
            gain(upx_v.at[level, d, kk], kk, z_at(NZ - d), 1 - x)
        if level == 0:
            need("d0c")
            d_relay[0].wait_recv()
        v_bf = acc[...].astype(bf)
        across = []
        for kk in range(2):
            ysend[level, kk] = dot32(v_bf, columns(level, (1 - y) * 2 + kk)).astype(bf)
            across.append(remote(ysend.at[level, kk], yrecv.at[level, kk], y_peer))
        mine = [dot32(v_bf, columns(level, y * 2 + kk)) for kk in range(2)]
        sols = []
        for kk in range(2):
            across[kk].wait_recv()
            sols.append(-(mine[kk] + yrecv[level, kk].astype(f32)))
            if level == 1:
                share(0, kk, sols[kk])
            else:
                finish(0, kk, sols[kk])
    for copy, away in stores:
        away.wait_recv()
        copy.wait()
    for copy in sent:
        copy.wait_send()


def fused_body(rhs, dinv, loff, targets):
    levels, rows, count = rhs.shape
    width = dinv.shape[2]
    links = targets.shape[1]
    half = count // 2
    bf = jnp.bfloat16
    f32 = jnp.float32
    any_space = pl.BlockSpec(memory_space=pl.ANY)
    pair = (2, rows, half)
    pair_t = (2, half, rows)
    return pl.pallas_call(
        fused_kernel,
        out_shape=jax.ShapeDtypeStruct(rhs.shape, f32),
        in_specs=[pl.BlockSpec(memory_space=pltpu.SMEM)] + [any_space] * 4,
        out_specs=any_space,
        scratch_shapes=[
            pltpu.VMEM((rows, count), f32),
            pltpu.VMEM((levels - 1,) + pair, f32),
            pltpu.VMEM((levels, 4, rows, width), bf),
            pltpu.VMEM((2, links, BLK, width), bf),
            pltpu.VMEM((2, links, BLK, width), bf),
            pltpu.VMEM((levels, 4, rows, half), bf),
            pltpu.VMEM((levels, 4, rows, half), bf),
            pltpu.VMEM((rows, half), bf),
            pltpu.VMEM((levels - 1,) + pair, f32),
            pltpu.VMEM((4,) + pair, f32),
            pltpu.VMEM((levels - 1, 4) + pair, bf),
            pltpu.VMEM((levels - 1, 4) + pair, bf),
            pltpu.VMEM((levels - 1, 4) + pair, bf),
            pltpu.VMEM((levels - 1, 4) + pair, bf),
            pltpu.VMEM((levels - 1, 4) + pair_t, bf),
            pltpu.VMEM((levels - 1, 4) + pair_t, bf),
            pltpu.VMEM((half, width), f32),
            pltpu.VMEM((levels - 1,) + pair_t, bf),
            pltpu.VMEM((levels - 1,) + pair_t, bf),
            pltpu.VMEM((levels,) + pair, f32),
            pltpu.VMEM((levels - 1, links), jnp.int32),
            pltpu.SMEM((levels - 1, links), jnp.int32),
            pltpu.SMEM((levels - 1, 2, links), jnp.int32),
            pltpu.SemaphoreType.DMA((20,)),
            pltpu.SemaphoreType.DMA((SENDS,)),
            pltpu.SemaphoreType.DMA((SENDS,)),
        ],
        compiler_params=pltpu.CompilerParams(
            collective_id=0, has_side_effects=True, vmem_limit_bytes=60 * 1024 * 1024
        ),
    )(targets, targets, rhs, dinv, loff.reshape(levels - 1, links, BLK, width))


def solution(mesh):
    in_specs = (
        P(None, ("snode", "col"), None),
        P(None, ("snode", "col"), None),
        P(None, ("snode", "col"), None),
        P(None, ("snode", "col")),
    )
    out_specs = P(None, ("snode", "col"), None)
    fits = mesh.shape["snode"] == 2 * NZ and mesh.shape["col"] == 4
    return jax.shard_map(
        fused_body if fits else body,
        mesh=mesh,
        in_specs=in_specs,
        out_specs=out_specs,
        check_vma=False,
    )
```

```python
import jax
import jax.numpy as jnp
from jax import lax
from jax.experimental import pallas as pl
from jax.experimental.pallas import tpu as pltpu
from jax.sharding import PartitionSpec as P

BLK = 128


def solve_block(matrix, resid_bf):
    return jnp.dot(
        matrix,
        lax.all_gather(resid_bf, "col", axis=0, tiled=True),
        preferred_element_type=jnp.float32,
    )


def route(update, links, col_rows):
    groups = lax.axis_size("snode")
    rhs_count = update.shape[1]
    flat = update.reshape(links.shape[0], BLK * rhs_count)
    count = groups * col_rows
    number = count // BLK
    wanted = 0 // BLK + lax.iota(jnp.int32, number)
    select = (wanted[:, None] == links[None, :]).astype(jnp.bfloat16)
    outgoing = (
        jnp.dot(select, flat, preferred_element_type=jnp.float32)
        .reshape(count, rhs_count)
        .astype(jnp.bfloat16)
        .reshape(groups, col_rows, rhs_count)
    )
    arrived = lax.all_to_all(outgoing, "snode", split_axis=0, concat_axis=0, tiled=True)
    return jnp.sum(arrived.astype(jnp.float32), axis=0)


def fetch(upper_bf, links):
    rhs_count = upper_bf.shape[1]
    gathered = lax.all_gather(upper_bf, "snode", axis=0, tiled=True)
    number = gathered.shape[0] // BLK
    wanted = lax.iota(jnp.int32, number)
    select = (links[:, None] == wanted[None, :]).astype(jnp.bfloat16)
    picked = jnp.dot(
        select, gathered.reshape(number, BLK * rhs_count), preferred_element_type=jnp.float32
    )
    return picked.astype(jnp.bfloat16).reshape(links.shape[0] * BLK, rhs_count)


def back_term(blocks, picked, col_rows):
    contract = (((0,), (0,)), ((), ()))

    def term(start, count):
        return lax.dot_general(blocks, picked, contract, preferred_element_type=jnp.float32)

    return lax.psum_scatter(
        term(jnp.int32(0), col_rows * lax.axis_size("col")).astype(jnp.bfloat16),
        "col",
        scatter_dimension=0,
        tiled=True,
    ).astype(jnp.float32)


def back_solve(matrix, reduced_bf, col_rows):
    contract = (((0,), (0,)), ((), ()))

    def term(start, count):
        return lax.dot_general(matrix, reduced_bf, contract, preferred_element_type=jnp.float32)

    return lax.psum_scatter(
        term(jnp.int32(0), col_rows * lax.axis_size("col")).astype(jnp.bfloat16),
        "col",
        scatter_dimension=0,
        tiled=True,
    ).astype(jnp.float32)


def body(rhs, dinv, loff, targets):
    levels = rhs.shape[0]
    col_rows = rhs.shape[1]
    rhs_count = rhs.shape[2]
    incoming = jnp.zeros((col_rows, rhs_count), jnp.float32)
    forward = []
    for level in range(levels):
        resid_bf = (rhs[level] - incoming).astype(jnp.bfloat16)
        solved = solve_block(dinv[level], resid_bf)
        forward.append(solved)
        if level + 1 < levels:
            solved_bf = solved.astype(jnp.bfloat16)
            full_bf = lax.all_gather(solved_bf, "col", axis=0, tiled=True)
            update = jnp.dot(loff[level], full_bf, preferred_element_type=jnp.float32).astype(
                jnp.bfloat16
            )
            incoming = route(update, targets[level], col_rows)
    outputs = [None] * levels
    upper_bf = None
    for level in reversed(range(levels)):
        reduced = forward[level]
        if level + 1 < levels:
            picked = fetch(upper_bf, targets[level])
            reduced = reduced - back_term(loff[level], picked, col_rows)
        solved = back_solve(dinv[level], reduced.astype(jnp.bfloat16), col_rows)
        outputs[level] = solved
        upper_bf = solved.astype(jnp.bfloat16)
    return jnp.stack(outputs)


NZ = 4
MESH_ID = pl.DeviceIdType.MESH
SENDS = 110
SLOTS = 48
PA = 2
PR = 1
ZS = (1, 3, 2)
STEPS = ((1, 0), (3, 0), (1, 1), (3, 1), (2, 0), (2, 1))
RSEQ = tuple((d, kk) for d in (2, 1, 3, 0) for kk in range(2))
ZSEQ = tuple((d, kk) for d in (2, 1, 3) for kk in range(2))


def dot32(a, b):
    return jnp.dot(a, b, preferred_element_type=jnp.float32)


def fused_kernel(
    targets_ref,
    targets_hbm,
    rhs_hbm,
    dinv_hbm,
    loff_hbm,
    out_hbm,
    rhs_0,
    rhs_v,
    d_v,
    loff_0,
    loff_1,
    r_v,
    f_v,
    stage,
    fwd_own,
    own_u,
    xsend,
    xrecv,
    zsend,
    zrecv,
    up_v,
    upx_v,
    acc,
    ysend,
    yrecv,
    out_v,
    peer_links_v,
    peer_links,
    inv_ref,
    local_sem,
    send_sem,
    recv_sem,
):
    bf = jnp.bfloat16
    f32 = jnp.float32
    rows = rhs_0.shape[0]
    half = r_v.shape[3]
    width = d_v.shape[3]
    s = lax.axis_index("snode")
    c = lax.axis_index("col")
    z, x = lax.div(s, 2), lax.rem(s, 2)
    y, k = lax.div(c, 2), lax.rem(c, 2)
    c_y = (1 - y) * 2 + k
    c_core = y * 2 + 1 - k
    y_peer = (s, c_y)
    core_peer = (s, c_core)
    diag_peer = (s, (1 - y) * 2 + 1 - k)
    x_peer = (z * 2 + 1 - x, c)
    own = pl.ds(y * 2, 2)
    lanes = pl.ds(pl.multiple_of(k * half, half), half)
    other = pl.ds(pl.multiple_of((1 - k) * half, half), half)

    def z_at(d):
        return lax.rem(z + d, NZ)

    def z_peer(d):
        return (z_at(d) * 2 + x, c)

    loads = {}
    waited = set()

    def load(name, src, dst):
        copy = pltpu.make_async_copy(src, dst, local_sem.at[len(loads)])
        copy.start()
        loads[name] = copy

    def need(*names):
        for name in names:
            if name not in waited:
                waited.add(name)
                if name in loads:
                    loads[name].wait()
                else:
                    pushed[name].wait_recv()

    load("rhs0", rhs_hbm.at[0], rhs_0)
    load("d0", dinv_hbm.at[0], d_v.at[0, c])
    load("loff0", loff_hbm.at[0], loff_0.at[k])
    load("d1", dinv_hbm.at[1], d_v.at[1, c])
    load("rhs1", rhs_hbm.at[1, :, lanes], rhs_v.at[0, k])
    load("rhs2", rhs_hbm.at[2, :, lanes], rhs_v.at[1, k])
    load("loff1", loff_hbm.at[1], loff_1.at[k])
    load("d2", dinv_hbm.at[2], d_v.at[2, c])

    barrier = pltpu.get_barrier_semaphore()
    peers = [y_peer, core_peer, diag_peer, x_peer, z_peer(1), z_peer(2), z_peer(3)]
    for peer in peers:
        pl.semaphore_signal(barrier, inc=1, device_id=peer, device_id_type=MESH_ID)
    need("rhs0")
    r_v[0, c] = rhs_0[:, lanes].astype(bf)
    stage[...] = rhs_0[:, other].astype(bf)
    pl.semaphore_wait(barrier, len(peers))

    sent = []
    slots = []
    free = set(range(SLOTS))
    pushed = {}

    def describe(src, dst, peer):
        at = len(sent)
        slot = min(free)
        free.remove(slot)
        copy = pltpu.make_async_remote_copy(
            src_ref=src,
            dst_ref=dst,
            send_sem=send_sem.at[slot],
            recv_sem=recv_sem.at[at],
            device_id=peer,
            device_id_type=MESH_ID,
        )
        sent.append(copy)
        slots.append(slot)
        return copy

    def remote(src, dst, peer):
        copy = describe(src, dst, peer)
        copy.start()
        return copy

    def push(name, src, dst):
        pushed[name] = remote(src, dst, core_peer)

    def to_y(buf, kk):
        return remote(buf.at[y * 2 + kk], buf.at[y * 2 + kk], y_peer)

    def pieces(src, dst, peer, count):
        size = src.shape[0] // count
        cuts = [pl.ds(at * size, size) for at in range(count)]
        return [(cut, remote(src.at[cut], dst.at[cut], peer)) for cut in cuts]

    def full(buf):
        return buf[...].reshape(4 * rows, half)

    def invert(level, kk, source):
        links = inv_ref.shape[2]
        entries = [source[level, at] for at in range(links)]
        for row in range(links):
            found = jnp.int32(0)
            for at, entry in enumerate(entries):
                found = jnp.where(entry == row, jnp.int32(at), found)
            inv_ref[level, kk, row] = found

    def link_rows(level, kk, zt, xt):
        group = (zt * 2 + xt) * 2
        loff_v = (loff_0, loff_1)[level]
        first = loff_v[kk, inv_ref[level, kk, group]]
        second = loff_v[kk, inv_ref[level, kk, group + 1]]
        return jnp.concatenate([first, second], axis=0)

    def columns(level, index):
        at = pl.multiple_of(index * rows, rows)
        return d_v[level, :, :, pl.ds(at, rows)].reshape(width, rows)

    first = [
        remote(r_v.at[0, c], r_v.at[0, c], y_peer),
        remote(stage, r_v.at[0, c], diag_peer),
        remote(stage, r_v.at[0, c], core_peer),
    ]
    push("d0c", dinv_hbm.at[0], d_v.at[0, c])
    push("links", targets_hbm, peer_links_v)
    push("loff0c", loff_hbm.at[0], loff_0.at[k])
    push("d1c", dinv_hbm.at[1], d_v.at[1, c])
    push("rhs1c", rhs_hbm.at[1, :, other], rhs_v.at[0, k])
    push("rhs2c", rhs_hbm.at[2, :, other], rhs_v.at[1, k])
    push("loff1c", loff_hbm.at[1], loff_1.at[k])
    push("d2c", dinv_hbm.at[2], d_v.at[2, c])

    d_y = {}
    d_relay = {}
    for level in (1, 2, 0):
        d_y[level] = describe(d_v.at[level, c], d_v.at[level, c], y_peer)
        d_relay[level] = describe(d_v.at[level, c_y], d_v.at[level, c_y], core_peer)

    def relay_d(level):
        d_y[level].wait_recv()
        d_relay[level].start()

    base = len(sent)
    stores = []
    settled = set()
    late = {id(d_y[0]), id(d_relay[0])}

    def settle(copies, outs):
        final = copies is sent
        for copy in copies:
            if id(copy) not in settled and (final or id(copy) not in late):
                settled.add(id(copy))
                copy.wait_send()
                free.add(slots[[other is copy for other in sent].index(True)])
        for copy, away in outs:
            if id(copy) not in settled:
                settled.add(id(copy))
                copy.wait()
                away.wait_recv()

    for level in range(2):
        invert(level, k, targets_ref)
    need("links")
    copy = pltpu.make_async_copy(peer_links_v, peer_links, local_sem.at[15])
    copy.start()
    copy.wait()
    for level in range(2):
        invert(level, 1 - k, peer_links)

    def route_sum(level, fwd_bf):
        mark = len(sent)
        arrivals = {}
        for d, kk in RSEQ:
            part = dot32(link_rows(level, kk, z_at(d), 1 - x), fwd_bf)
            xsend[level, d, kk] = part.astype(bf)
            arrivals[d, kk] = pieces(
                xsend.at[level, d, kk], xrecv.at[level, d, kk], x_peer, PR
            )
        for d, kk in RSEQ:
            own_u[d, kk] = dot32(link_rows(level, kk, z_at(d), x), fwd_bf)
        need("rhs%d" % (level + 1), "rhs%dc" % (level + 1))
        settle((list(pushed.values()) if level else first) + sent[base:mark], [])
        landed = {}
        for d, kk in RSEQ:
            landed[d, kk] = []
            for cut, copy in arrivals[d, kk]:
                copy.wait_recv()
                both = own_u[d, kk, cut] + xrecv[level, d, kk, cut].astype(f32)
                if d == 0:
                    own_u[0, kk, cut] = rhs_v[level, kk, cut] - both
                    continue
                zsend[level, d, kk, cut] = both.astype(bf)
                src, dst = zsend.at[level, d, kk, cut], zrecv.at[level, d, kk, cut]
                landed[d, kk].append((cut, remote(src, dst, z_peer(d))))
        gathers = []
        left = [3, 3]
        for d, kk in ZSEQ:
            left[kk] -= 1
            for cut, copy in landed[d, kk]:
                copy.wait_recv()
                resid = own_u[0, kk, cut] - zrecv[level, d, kk, cut].astype(f32)
                if left[kk]:
                    own_u[0, kk, cut] = resid
                else:
                    r_v[level + 1, y * 2 + kk, cut] = resid.astype(bf)
                    row = r_v.at[level + 1, y * 2 + kk, cut]
                    gathers.append(remote(row, row, y_peer))
        return gathers

    for copy in first:
        copy.wait_recv()
    need("d0", "d0c")
    resid = full(r_v.at[0])
    gathers = []
    for kk in range(2):
        part = dot32(d_v[0, y * 2 + kk], resid)
        fwd_own[0, kk] = part
        f_v[0, y * 2 + kk] = part.astype(bf)
        gathers.append(to_y(f_v.at[0], kk))
    need("d1")
    d_y[1].start()
    need("loff0", "loff0c")
    for copy in gathers:
        copy.wait_recv()
    gathers = route_sum(0, full(f_v.at[0]))

    need("loff1", "loff1c", "d1c", "d2")
    d_y[2].start()
    relay_d(1)
    for copy in gathers:
        copy.wait_recv()
    d_relay[1].wait_recv()
    resid = full(r_v.at[1])
    for i in range(4):
        f_v[1, i] = dot32(d_v[1, i], resid).astype(bf)
    gathers = route_sum(1, full(f_v.at[1]))

    need("d2c")
    d_y[0].start()
    relay_d(2)
    resid = full(r_v.at[1])
    for kk in range(2):
        fwd_own[1, kk] = dot32(d_v[1, y * 2 + kk], resid)
    for copy in gathers:
        copy.wait_recv()
    d_relay[2].wait_recv()
    resid = full(r_v.at[2])
    for i in range(4):
        f_v[2, i] = dot32(d_v[2, i], resid).astype(bf)

    def finish(level, kk, sol_t):
        if kk == 0:
            src, dst = out_v.at[level], out_hbm.at[level, :, lanes]
            copy = pltpu.make_async_copy(src.at[k], dst, local_sem.at[16 + level])
            stores.append((copy, describe(src.at[1 - k], dst, core_peer)))
        out_v[level, kk] = sol_t.T
        copy, away = stores[-1]
        pl.when(k == kk)(copy.start)
        pl.when(k != kk)(away.start)

    from_x = {}
    from_z = {}

    def share(level, kk, sol_t):
        up_v[level, 0, kk] = sol_t.astype(bf)
        own_up = up_v.at[level, 0, kk]
        from_x[level, 0, kk] = [remote(own_up, upx_v.at[level, 0, kk], x_peer)]
        for d in ZS:
            from_z[level, d, kk] = pieces(own_up, up_v.at[level, d, kk], z_peer(d), PA)

    mark = len(sent)
    sols = []
    for kk in range(2):
        sols.append(
            lax.dot_general(
                full(f_v.at[2]),
                columns(2, y * 2 + kk),
                (((0,), (0,)), ((), ())),
                preferred_element_type=f32,
            )
        )
        share(1, kk, sols[kk])
    for level in (1, 0):
        for kk in range(2):
            finish(level + 1, kk, sols[kk])
        acc[...] = jnp.zeros((half, width), f32)
        at = pl.multiple_of(y * 2 * rows, 2 * rows)
        acc[:, pl.ds(at, 2 * rows)] = -(fwd_own[level].reshape(2 * rows, half).T)

        def gain(buf, kk, zt, xt):
            acc[...] += dot32(buf[...], link_rows(level, kk, zt, xt))

        for kk in range(2):
            gain(up_v.at[level, 0, kk], kk, z, x)
        if level == 0:
            settle(sent[:before], stores[:-1])
        else:
            settle(sent[base:mark] + [d_y[1], d_relay[1]], [])
        for d, kk in STEPS:
            from_x[level, d, kk] = []
            for cut, copy in from_z[level, d, kk]:
                copy.wait_recv()
                src, dst = up_v.at[level, d, kk, cut], upx_v.at[level, d, kk, cut]
                from_x[level, d, kk].append(remote(src, dst, x_peer))
            gain(up_v.at[level, d, kk], kk, z_at(NZ - d), x)
        if level == 0:
            relay_d(0)
            settle(sent[:-1], [])
        for d, kk in ((0, 0), (0, 1)) + STEPS:
            for copy in from_x[level, d, kk]:
                copy.wait_recv()
            gain(upx_v.at[level, d, kk], kk, z_at(NZ - d), 1 - x)
        if level == 0:
            need("d0c")
            d_relay[0].wait_recv()
        v_bf = acc[...].astype(bf)
        across = []
        for kk in range(2):
            ysend[level, kk] = dot32(v_bf, columns(level, (1 - y) * 2 + kk)).astype(bf)
            across.append(remote(ysend.at[level, kk], yrecv.at[level, kk], y_peer))
        mine = [dot32(v_bf, columns(level, y * 2 + kk)) for kk in range(2)]
        sols = []
        before = len(sent)
        for kk in range(2):
            across[kk].wait_recv()
            sols.append(-(mine[kk] + yrecv[level, kk].astype(f32)))
            if level == 1:
                share(0, kk, sols[kk])
            else:
                finish(0, kk, sols[kk])
    settle(sent, stores)


def fused_body(rhs, dinv, loff, targets):
    levels, rows, count = rhs.shape
    width = dinv.shape[2]
    links = targets.shape[1]
    half = count // 2
    bf = jnp.bfloat16
    f32 = jnp.float32
    any_space = pl.BlockSpec(memory_space=pl.ANY)
    pair = (2, rows, half)
    pair_t = (2, half, rows)
    return pl.pallas_call(
        fused_kernel,
        out_shape=jax.ShapeDtypeStruct(rhs.shape, f32),
        in_specs=[pl.BlockSpec(memory_space=pltpu.SMEM)] + [any_space] * 4,
        out_specs=any_space,
        scratch_shapes=[
            pltpu.VMEM((rows, count), f32),
            pltpu.VMEM((levels - 1,) + pair, f32),
            pltpu.VMEM((levels, 4, rows, width), bf),
            pltpu.VMEM((2, links, BLK, width), bf),
            pltpu.VMEM((2, links, BLK, width), bf),
            pltpu.VMEM((levels, 4, rows, half), bf),
            pltpu.VMEM((levels, 4, rows, half), bf),
            pltpu.VMEM((rows, half), bf),
            pltpu.VMEM((levels - 1,) + pair, f32),
            pltpu.VMEM((4,) + pair, f32),
            pltpu.VMEM((levels - 1, 4) + pair, bf),
            pltpu.VMEM((levels - 1, 4) + pair, bf),
            pltpu.VMEM((levels - 1, 4) + pair, bf),
            pltpu.VMEM((levels - 1, 4) + pair, bf),
            pltpu.VMEM((levels - 1, 4) + pair_t, bf),
            pltpu.VMEM((levels - 1, 4) + pair_t, bf),
            pltpu.VMEM((half, width), f32),
            pltpu.VMEM((levels - 1,) + pair_t, bf),
            pltpu.VMEM((levels - 1,) + pair_t, bf),
            pltpu.VMEM((levels,) + pair, f32),
            pltpu.VMEM((levels - 1, links), jnp.int32),
            pltpu.SMEM((levels - 1, links), jnp.int32),
            pltpu.SMEM((levels - 1, 2, links), jnp.int32),
            pltpu.SemaphoreType.DMA((20,)),
            pltpu.SemaphoreType.DMA((SLOTS,)),
            pltpu.SemaphoreType.DMA((SENDS,)),
        ],
        compiler_params=pltpu.CompilerParams(
            collective_id=0, has_side_effects=True, vmem_limit_bytes=60 * 1024 * 1024
        ),
    )(targets, targets, rhs, dinv, loff.reshape(levels - 1, links, BLK, width))


def solution(mesh):
    in_specs = (
        P(None, ("snode", "col"), None),
        P(None, ("snode", "col"), None),
        P(None, ("snode", "col"), None),
        P(None, ("snode", "col")),
    )
    out_specs = P(None, ("snode", "col"), None)
    fits = mesh.shape["snode"] == 2 * NZ and mesh.shape["col"] == 4
    return jax.shard_map(
        fused_body if fits else body,
        mesh=mesh,
        in_specs=in_specs,
        out_specs=out_specs,
        check_vma=False,
    )
```

```python
import jax
import jax.numpy as jnp
from jax import lax
from jax.experimental import pallas as pl
from jax.experimental.pallas import tpu as pltpu
from jax.sharding import PartitionSpec as P

BLK = 128


def solve_block(matrix, resid_bf):
    return jnp.dot(
        matrix,
        lax.all_gather(resid_bf, "col", axis=0, tiled=True),
        preferred_element_type=jnp.float32,
    )


def route(update, links, col_rows):
    groups = lax.axis_size("snode")
    rhs_count = update.shape[1]
    flat = update.reshape(links.shape[0], BLK * rhs_count)
    count = groups * col_rows
    number = count // BLK
    wanted = 0 // BLK + lax.iota(jnp.int32, number)
    select = (wanted[:, None] == links[None, :]).astype(jnp.bfloat16)
    outgoing = (
        jnp.dot(select, flat, preferred_element_type=jnp.float32)
        .reshape(count, rhs_count)
        .astype(jnp.bfloat16)
        .reshape(groups, col_rows, rhs_count)
    )
    arrived = lax.all_to_all(outgoing, "snode", split_axis=0, concat_axis=0, tiled=True)
    return jnp.sum(arrived.astype(jnp.float32), axis=0)


def fetch(upper_bf, links):
    rhs_count = upper_bf.shape[1]
    gathered = lax.all_gather(upper_bf, "snode", axis=0, tiled=True)
    number = gathered.shape[0] // BLK
    wanted = lax.iota(jnp.int32, number)
    select = (links[:, None] == wanted[None, :]).astype(jnp.bfloat16)
    picked = jnp.dot(
        select, gathered.reshape(number, BLK * rhs_count), preferred_element_type=jnp.float32
    )
    return picked.astype(jnp.bfloat16).reshape(links.shape[0] * BLK, rhs_count)


def back_term(blocks, picked, col_rows):
    contract = (((0,), (0,)), ((), ()))

    def term(start, count):
        return lax.dot_general(blocks, picked, contract, preferred_element_type=jnp.float32)

    return lax.psum_scatter(
        term(jnp.int32(0), col_rows * lax.axis_size("col")).astype(jnp.bfloat16),
        "col",
        scatter_dimension=0,
        tiled=True,
    ).astype(jnp.float32)


def back_solve(matrix, reduced_bf, col_rows):
    contract = (((0,), (0,)), ((), ()))

    def term(start, count):
        return lax.dot_general(matrix, reduced_bf, contract, preferred_element_type=jnp.float32)

    return lax.psum_scatter(
        term(jnp.int32(0), col_rows * lax.axis_size("col")).astype(jnp.bfloat16),
        "col",
        scatter_dimension=0,
        tiled=True,
    ).astype(jnp.float32)


def body(rhs, dinv, loff, targets):
    levels = rhs.shape[0]
    col_rows = rhs.shape[1]
    rhs_count = rhs.shape[2]
    incoming = jnp.zeros((col_rows, rhs_count), jnp.float32)
    forward = []
    for level in range(levels):
        resid_bf = (rhs[level] - incoming).astype(jnp.bfloat16)
        solved = solve_block(dinv[level], resid_bf)
        forward.append(solved)
        if level + 1 < levels:
            solved_bf = solved.astype(jnp.bfloat16)
            full_bf = lax.all_gather(solved_bf, "col", axis=0, tiled=True)
            update = jnp.dot(loff[level], full_bf, preferred_element_type=jnp.float32).astype(
                jnp.bfloat16
            )
            incoming = route(update, targets[level], col_rows)
    outputs = [None] * levels
    upper_bf = None
    for level in reversed(range(levels)):
        reduced = forward[level]
        if level + 1 < levels:
            picked = fetch(upper_bf, targets[level])
            reduced = reduced - back_term(loff[level], picked, col_rows)
        solved = back_solve(dinv[level], reduced.astype(jnp.bfloat16), col_rows)
        outputs[level] = solved
        upper_bf = solved.astype(jnp.bfloat16)
    return jnp.stack(outputs)


NZ = 4
MESH_ID = pl.DeviceIdType.MESH
SENDS = 94
SLOTS = 48
PA = 2
PR = 1
ZS = (1, 3, 2)
STEPS = ((1, 0), (3, 0), (1, 1), (3, 1), (2, 0), (2, 1))
RSEQ = tuple((d, kk) for d in (2, 1, 3, 0) for kk in range(2))
ZSEQ = tuple((d, kk) for d in (2, 1, 3) for kk in range(2))


def dot32(a, b):
    return jnp.dot(a, b, preferred_element_type=jnp.float32)


def fused_kernel(
    targets_ref,
    targets_hbm,
    rhs_hbm,
    dinv_hbm,
    loff_hbm,
    out_hbm,
    rhs_0,
    rhs_v,
    d_v,
    loff_0,
    loff_1,
    r_v,
    f_v,
    stage,
    fwd_own,
    own_u,
    xsend,
    xrecv,
    zsend,
    zrecv,
    up_v,
    upx_v,
    acc,
    ysend,
    yrecv,
    out_v,
    peer_links_v,
    peer_links,
    inv_ref,
    local_sem,
    send_sem,
    recv_sem,
):
    bf = jnp.bfloat16
    f32 = jnp.float32
    rows = rhs_0.shape[0]
    half = r_v.shape[3]
    width = d_v.shape[3]
    s = lax.axis_index("snode")
    c = lax.axis_index("col")
    z, x = lax.div(s, 2), lax.rem(s, 2)
    y, k = lax.div(c, 2), lax.rem(c, 2)
    c_y = (1 - y) * 2 + k
    c_core = y * 2 + 1 - k
    y_peer = (s, c_y)
    core_peer = (s, c_core)
    diag_peer = (s, (1 - y) * 2 + 1 - k)
    x_peer = (z * 2 + 1 - x, c)
    own = pl.ds(y * 2, 2)
    lanes = pl.ds(pl.multiple_of(k * half, half), half)
    other = pl.ds(pl.multiple_of((1 - k) * half, half), half)

    def z_at(d):
        return lax.rem(z + d, NZ)

    def z_peer(d):
        return (z_at(d) * 2 + x, c)

    loads = {}
    waited = set()

    def load(name, src, dst):
        copy = pltpu.make_async_copy(src, dst, local_sem.at[len(loads)])
        copy.start()
        loads[name] = copy

    def need(*names):
        for name in names:
            if name not in waited:
                waited.add(name)
                if name in loads:
                    loads[name].wait()
                else:
                    pushed[name].wait_recv()

    load("rhs0", rhs_hbm.at[0], rhs_0)
    load("d0", dinv_hbm.at[0], d_v.at[0, c])
    load("loff0", loff_hbm.at[0], loff_0.at[k])
    load("d1", dinv_hbm.at[1], d_v.at[1, c])
    load("rhs1", rhs_hbm.at[1, :, lanes], rhs_v.at[0, k])
    load("rhs2", rhs_hbm.at[2, :, lanes], rhs_v.at[1, k])
    load("loff1", loff_hbm.at[1], loff_1.at[k])
    load("d2", dinv_hbm.at[2], d_v.at[2, c])

    barrier = pltpu.get_barrier_semaphore()
    peers = [y_peer, core_peer, diag_peer, x_peer, z_peer(1), z_peer(2), z_peer(3)]
    for peer in peers:
        pl.semaphore_signal(barrier, inc=1, device_id=peer, device_id_type=MESH_ID)
    need("rhs0")
    r_v[0, c] = rhs_0[:, lanes].astype(bf)
    stage[...] = rhs_0[:, other].astype(bf)
    pl.semaphore_wait(barrier, len(peers))

    sent = []
    slots = []
    free = set(range(SLOTS))
    pushed = {}

    def describe(src, dst, peer):
        at = len(sent)
        slot = min(free)
        free.remove(slot)
        copy = pltpu.make_async_remote_copy(
            src_ref=src,
            dst_ref=dst,
            send_sem=send_sem.at[slot],
            recv_sem=recv_sem.at[at],
            device_id=peer,
            device_id_type=MESH_ID,
        )
        sent.append(copy)
        slots.append(slot)
        return copy

    def remote(src, dst, peer):
        copy = describe(src, dst, peer)
        copy.start()
        return copy

    def push(name, src, dst):
        pushed[name] = remote(src, dst, core_peer)

    def to_y(buf, kk):
        return remote(buf.at[y * 2 + kk], buf.at[y * 2 + kk], y_peer)

    def pieces(src, dst, peer, count):
        size = src.shape[0] // count
        cuts = [pl.ds(at * size, size) for at in range(count)]
        return [(cut, remote(src.at[cut], dst.at[cut], peer)) for cut in cuts]

    def full(buf):
        return buf[...].reshape(4 * rows, half)

    def invert(level, kk, source):
        links = inv_ref.shape[2]
        entries = [source[level, at] for at in range(links)]
        for row in range(links):
            found = jnp.int32(0)
            for at, entry in enumerate(entries):
                found = jnp.where(entry == row, jnp.int32(at), found)
            inv_ref[level, kk, row] = found

    def link_rows(level, kk, zt, xt):
        group = (zt * 2 + xt) * 2
        loff_v = (loff_0, loff_1)[level]
        first = loff_v[kk, inv_ref[level, kk, group]]
        second = loff_v[kk, inv_ref[level, kk, group + 1]]
        return jnp.concatenate([first, second], axis=0)

    def columns(level, index):
        at = pl.multiple_of(index * rows, rows)
        return d_v[level, :, :, pl.ds(at, rows)].reshape(width, rows)

    first = [
        remote(r_v.at[0, c], r_v.at[0, c], y_peer),
        remote(stage, r_v.at[0, c], diag_peer),
        remote(stage, r_v.at[0, c], core_peer),
    ]
    push("d0c", dinv_hbm.at[0], d_v.at[0, c])
    push("links", targets_hbm, peer_links_v)
    push("loff0c", loff_hbm.at[0], loff_0.at[k])
    push("d1c", dinv_hbm.at[1], d_v.at[1, c])
    push("rhs1c", rhs_hbm.at[1, :, other], rhs_v.at[0, k])
    push("rhs2c", rhs_hbm.at[2, :, other], rhs_v.at[1, k])
    push("loff1c", loff_hbm.at[1], loff_1.at[k])
    push("d2c", dinv_hbm.at[2], d_v.at[2, c])

    d_y = {}
    d_relay = {}
    for level in (1, 2, 0):
        d_y[level] = describe(d_v.at[level, c], d_v.at[level, c], y_peer)
        d_relay[level] = describe(d_v.at[level, c_y], d_v.at[level, c_y], core_peer)

    def relay_d(level):
        d_y[level].wait_recv()
        d_relay[level].start()

    base = len(sent)
    stores = []
    settled = set()
    late = {id(d_y[0]), id(d_relay[0])}

    def settle(copies, outs):
        final = copies is sent
        for copy in copies:
            if id(copy) not in settled and (final or id(copy) not in late):
                settled.add(id(copy))
                copy.wait_send()
                free.add(slots[[other is copy for other in sent].index(True)])
        for copy, away in outs:
            if id(copy) not in settled:
                settled.add(id(copy))
                copy.wait()
                away.wait_recv()

    for level in range(2):
        invert(level, k, targets_ref)
    need("links")
    copy = pltpu.make_async_copy(peer_links_v, peer_links, local_sem.at[15])
    copy.start()
    copy.wait()
    for level in range(2):
        invert(level, 1 - k, peer_links)

    def route_sum(level, fwd_bf):
        mark = len(sent)
        arrivals = {}
        for d, kk in RSEQ:
            part = dot32(link_rows(level, kk, z_at(d), 1 - x), fwd_bf)
            xsend[level, d, kk] = part.astype(bf)
            arrivals[d, kk] = pieces(
                xsend.at[level, d, kk], xrecv.at[level, d, kk], x_peer, PR
            )
        for d, kk in RSEQ:
            own_u[d, kk] = dot32(link_rows(level, kk, z_at(d), x), fwd_bf)
        need("rhs%d" % (level + 1), "rhs%dc" % (level + 1))
        settle((list(pushed.values()) if level else first) + sent[base:mark], [])
        landed = {}
        for d, kk in RSEQ:
            landed[d, kk] = []
            for cut, copy in arrivals[d, kk]:
                copy.wait_recv()
                both = own_u[d, kk, cut] + xrecv[level, d, kk, cut].astype(f32)
                if d == 0:
                    own_u[0, kk, cut] = rhs_v[level, kk, cut] - both
                    continue
                zsend[level, d, kk, cut] = both.astype(bf)
                src, dst = zsend.at[level, d, kk, cut], zrecv.at[level, d, kk, cut]
                landed[d, kk].append((cut, remote(src, dst, z_peer(d))))
        gathers = []
        left = [3, 3]
        for d, kk in ZSEQ:
            left[kk] -= 1
            for cut, copy in landed[d, kk]:
                copy.wait_recv()
                resid = own_u[0, kk, cut] - zrecv[level, d, kk, cut].astype(f32)
                if left[kk]:
                    own_u[0, kk, cut] = resid
                else:
                    r_v[level + 1, y * 2 + kk, cut] = resid.astype(bf)
                    row = r_v.at[level + 1, y * 2 + kk, cut]
                    gathers.append(remote(row, row, y_peer))
        return gathers

    for copy in first:
        copy.wait_recv()
    need("d0", "d0c")
    resid = full(r_v.at[0])
    gathers = []
    for kk in range(2):
        part = dot32(d_v[0, y * 2 + kk], resid)
        fwd_own[0, kk] = part
        f_v[0, y * 2 + kk] = part.astype(bf)
        gathers.append(to_y(f_v.at[0], kk))
    need("d1")
    d_y[1].start()
    need("loff0", "loff0c")
    for copy in gathers:
        copy.wait_recv()
    gathers = route_sum(0, full(f_v.at[0]))

    need("loff1", "loff1c", "d1c", "d2")
    d_y[2].start()
    relay_d(1)
    for copy in gathers:
        copy.wait_recv()
    d_relay[1].wait_recv()
    resid = full(r_v.at[1])
    for i in range(4):
        f_v[1, i] = dot32(d_v[1, i], resid).astype(bf)
    gathers = route_sum(1, full(f_v.at[1]))

    need("d2c")
    d_y[0].start()
    relay_d(2)
    resid = full(r_v.at[1])
    for kk in range(2):
        fwd_own[1, kk] = dot32(d_v[1, y * 2 + kk], resid)
    for copy in gathers:
        copy.wait_recv()
    d_relay[2].wait_recv()
    resid = full(r_v.at[2])
    for i in range(4):
        f_v[2, i] = dot32(d_v[2, i], resid).astype(bf)

    def finish(level, kk, sol_t):
        if kk == 0:
            src, dst = out_v.at[level], out_hbm.at[level, :, lanes]
            copy = pltpu.make_async_copy(src.at[k], dst, local_sem.at[16 + level])
            stores.append((copy, describe(src.at[1 - k], dst, core_peer)))
        out_v[level, kk] = sol_t.T
        copy, away = stores[-1]
        pl.when(k == kk)(copy.start)
        pl.when(k != kk)(away.start)

    from_x = {}
    from_z = {}

    def share(level, kk, sol_t):
        up_v[level, 0, kk] = sol_t.astype(bf)
        own_up = up_v.at[level, 0, kk]
        from_x[level, 0, kk] = [remote(own_up, upx_v.at[level, 0, kk], x_peer)]
        for d in ZS:
            from_z[level, d, kk] = pieces(
                own_up, up_v.at[level, d, kk], z_peer(d), PA if d == 2 else 1
            )

    mark = len(sent)
    sols = []
    for kk in range(2):
        sols.append(
            lax.dot_general(
                full(f_v.at[2]),
                columns(2, y * 2 + kk),
                (((0,), (0,)), ((), ())),
                preferred_element_type=f32,
            )
        )
        share(1, kk, sols[kk])
    for level in (1, 0):
        for kk in range(2):
            finish(level + 1, kk, sols[kk])
        acc[...] = jnp.zeros((half, width), f32)
        at = pl.multiple_of(y * 2 * rows, 2 * rows)
        acc[:, pl.ds(at, 2 * rows)] = -(fwd_own[level].reshape(2 * rows, half).T)

        def gain(buf, kk, zt, xt):
            acc[...] += dot32(buf[...], link_rows(level, kk, zt, xt))

        for kk in range(2):
            gain(up_v.at[level, 0, kk], kk, z, x)
        if level == 0:
            settle(sent[:before], stores[:-1])
        else:
            settle(sent[base:mark] + [d_y[1], d_relay[1]], [])
        for d, kk in STEPS:
            from_x[level, d, kk] = []
            for cut, copy in from_z[level, d, kk]:
                copy.wait_recv()
                src, dst = up_v.at[level, d, kk, cut], upx_v.at[level, d, kk, cut]
                from_x[level, d, kk].append(remote(src, dst, x_peer))
            gain(up_v.at[level, d, kk], kk, z_at(NZ - d), x)
        if level == 0:
            relay_d(0)
            settle(sent[:-1], [])
        for d, kk in ((0, 0), (0, 1)) + STEPS:
            for copy in from_x[level, d, kk]:
                copy.wait_recv()
            gain(upx_v.at[level, d, kk], kk, z_at(NZ - d), 1 - x)
        if level == 0:
            need("d0c")
            d_relay[0].wait_recv()
        v_bf = acc[...].astype(bf)
        across = []
        for kk in range(2):
            ysend[level, kk] = dot32(v_bf, columns(level, (1 - y) * 2 + kk)).astype(bf)
            across.append(remote(ysend.at[level, kk], yrecv.at[level, kk], y_peer))
        mine = [dot32(v_bf, columns(level, y * 2 + kk)) for kk in range(2)]
        sols = []
        before = len(sent)
        for kk in range(2):
            across[kk].wait_recv()
            sols.append(-(mine[kk] + yrecv[level, kk].astype(f32)))
            if level == 1:
                share(0, kk, sols[kk])
            else:
                finish(0, kk, sols[kk])
    settle(sent, stores)


def fused_body(rhs, dinv, loff, targets):
    levels, rows, count = rhs.shape
    width = dinv.shape[2]
    links = targets.shape[1]
    half = count // 2
    bf = jnp.bfloat16
    f32 = jnp.float32
    any_space = pl.BlockSpec(memory_space=pl.ANY)
    pair = (2, rows, half)
    pair_t = (2, half, rows)
    return pl.pallas_call(
        fused_kernel,
        out_shape=jax.ShapeDtypeStruct(rhs.shape, f32),
        in_specs=[pl.BlockSpec(memory_space=pltpu.SMEM)] + [any_space] * 4,
        out_specs=any_space,
        scratch_shapes=[
            pltpu.VMEM((rows, count), f32),
            pltpu.VMEM((levels - 1,) + pair, f32),
            pltpu.VMEM((levels, 4, rows, width), bf),
            pltpu.VMEM((2, links, BLK, width), bf),
            pltpu.VMEM((2, links, BLK, width), bf),
            pltpu.VMEM((levels, 4, rows, half), bf),
            pltpu.VMEM((levels, 4, rows, half), bf),
            pltpu.VMEM((rows, half), bf),
            pltpu.VMEM((levels - 1,) + pair, f32),
            pltpu.VMEM((4,) + pair, f32),
            pltpu.VMEM((levels - 1, 4) + pair, bf),
            pltpu.VMEM((levels - 1, 4) + pair, bf),
            pltpu.VMEM((levels - 1, 4) + pair, bf),
            pltpu.VMEM((levels - 1, 4) + pair, bf),
            pltpu.VMEM((levels - 1, 4) + pair_t, bf),
            pltpu.VMEM((levels - 1, 4) + pair_t, bf),
            pltpu.VMEM((half, width), f32),
            pltpu.VMEM((levels - 1,) + pair_t, bf),
            pltpu.VMEM((levels - 1,) + pair_t, bf),
            pltpu.VMEM((levels,) + pair, f32),
            pltpu.VMEM((levels - 1, links), jnp.int32),
            pltpu.SMEM((levels - 1, links), jnp.int32),
            pltpu.SMEM((levels - 1, 2, links), jnp.int32),
            pltpu.SemaphoreType.DMA((20,)),
            pltpu.SemaphoreType.DMA((SLOTS,)),
            pltpu.SemaphoreType.DMA((SENDS,)),
        ],
        compiler_params=pltpu.CompilerParams(
            collective_id=0, has_side_effects=True, vmem_limit_bytes=60 * 1024 * 1024
        ),
    )(targets, targets, rhs, dinv, loff.reshape(levels - 1, links, BLK, width))


def solution(mesh):
    in_specs = (
        P(None, ("snode", "col"), None),
        P(None, ("snode", "col"), None),
        P(None, ("snode", "col"), None),
        P(None, ("snode", "col")),
    )
    out_specs = P(None, ("snode", "col"), None)
    fits = mesh.shape["snode"] == 2 * NZ and mesh.shape["col"] == 4
    return jax.shard_map(
        fused_body if fits else body,
        mesh=mesh,
        in_specs=in_specs,
        out_specs=out_specs,
        check_vma=False,
    )
```
